32 devices in a mesh: gx: 2 (over x), gy: 4 (over y, core), sa: 4 (over z).
Axes of the slice: x: 2, y: 2, z: 4, core: 2. Of those that a mesh axis runs over, the one named last changes fastest.
Arguments:
- start_field: float32 [512, 2048], P('gx', 'gy'), may hold values from -6 to 6
- base_coef: float32 [512, 2048], P('gx', 'gy'), may hold values from 0.03 to 0.1
- region: int32 [512, 2048], P('gx', 'gy'), may hold values from 0 to 5
- codes_a: int32 [16, 6], P('sa'), may hold values from 0 to 1048575
- codes_b: int32 [16, 6], P('sa'), may hold values from 0 to 1048575
Outputs:
- first_order: float32 [6, 512, 2048], P(None, 'gx', ('gy', 'sa'))
- total_order: float32 [6, 512, 2048], P(None, 'gx', ('gy', 'sa'))
- aggregate: float32 [2, 6], replicated
The draws below stay inside these ranges and needn't reach their ends.
All inputs are finite; a program needn't handle non-finite values.
Results may differ from the reference program's by a relative error of at most 0.0003.
Values sent between devices are 32-bit elements; how exact they have to be, the bound alone decides.
No kernel may reach another device: no remote copies, remote signals or barrier semaphores. Data moves between devices by JAX's collectives and lax.ppermute only.
A program may use at most 192 MiB of HBM per device.

```python
import math
import jax
import jax.numpy as jnp
from jax import lax

P_SIZE = 6
STEPS = 3
B = 16
NX = 512
NY = 2048


def plant(result, own_key, low, largest):
    longest = result.shape.index(max(result.shape))
    spots = []
    for shift in (0, 1):
        where = [jax.random.randint(jax.random.fold_in(own_key, axis), (), 0, length) for axis, length in enumerate(result.shape)]
        where[longest] = (where[longest] + shift) % result.shape[longest]
        spots.append(tuple(where))
    return result.at[spots[0]].set(low).at[spots[1]].set(largest)


def levels(rng, shape, cuts, least, high):
    def one(axis_at, blocks):
        heights = jax.random.uniform(jax.random.fold_in(jax.random.fold_in(rng, 6), axis_at), (blocks,), jnp.float32, least / len(cuts), high / len(cuts))
        return jnp.repeat(jnp.exp(heights), shape[axis_at] // blocks).reshape((-1,) + (1,) * (len(shape) - axis_at - 1))

    level = one(*cuts[0])
    for cut in cuts[1:]:
        level = level * one(*cut)
    return level


def scatter_about(rng, extent, deviation, limit, pieces=(), dtype=jnp.bfloat16):
    values = deviation * jax.random.normal(rng, extent, jnp.float32)
    if pieces:
        values = values * levels(rng, extent, pieces, -0.22, 0.18)
    return jnp.clip(values, -limit, limit).astype(dtype)


def setup_inputs(seed: int = 0) -> dict:
    key_of = jax.random.split(jax.random.key(seed), 6)
    return {
        "start_field": scatter_about(key_of[0], (NX, NY), 1.0, 6.0, ((0, 2), (1, 4)), jnp.float32),
        "base_coef": jnp.clip(jnp.exp(math.log(0.1) - 1.2039728 * jax.random.uniform(key_of[1], (NX, NY), jnp.float32) ** levels(key_of[1], (NX, NY), ((0, 2), (1, 4)), -0.2, 0.2)), 0.03, 0.1),
        "region": plant(jax.random.randint(key_of[2], (NX, NY), 0, P_SIZE), jax.random.fold_in(key_of[2], 1), 0, P_SIZE - 1).astype(jnp.int32),
        "codes_a": plant(jax.random.randint(key_of[3], (B, P_SIZE), 0, 1048576), jax.random.fold_in(key_of[3], 1), 0, 1048575).astype(jnp.int32),
        "codes_b": plant(jax.random.randint(key_of[4], (B, P_SIZE), 0, 1048576), jax.random.fold_in(key_of[4], 1), 0, 1048575).astype(jnp.int32),
    }


code_scale = 1048576.0
lowest = 0.5
spread = 1.9
var_floor = 0.02


def run_params(rows_a, rows_b):
    first_set = lowest + spread * rows_a.astype(jnp.float32) / code_scale
    second_set = lowest + spread * rows_b.astype(jnp.float32) / code_scale
    picks = jnp.arange(P_SIZE)[:, None] == jnp.arange(P_SIZE)[None, :]
    mixed = jnp.where(picks, second_set[..., None, :], first_set[..., None, :])
    return jnp.concatenate([first_set[..., None, :], second_set[..., None, :], mixed], axis=-2)


def diffuse(padded_field, padded_coef):
    centre = padded_field[:, 1:-1, 1:-1]
    centre_coef = padded_coef[:, 1:-1, 1:-1]
    flux = jnp.zeros_like(centre)
    for near_field, near_coef in ((padded_field[:, 2:, 1:-1], padded_coef[:, 2:, 1:-1]),
                                  (padded_field[:, :-2, 1:-1], padded_coef[:, :-2, 1:-1]),
                                  (padded_field[:, 1:-1, 2:], padded_coef[:, 1:-1, 2:]),
                                  (padded_field[:, 1:-1, :-2], padded_coef[:, 1:-1, :-2])):
        flux = flux + (centre_coef + near_coef) * (near_field - centre)
    return centre + 0.5 * flux


def partial_sums(fields):
    first_f = fields[0]
    second_f = fields[1]
    mixed_f = fields[2:]
    level_sum = jnp.sum(first_f + second_f, axis=0)
    square_sum = jnp.sum(first_f * first_f + second_f * second_f, axis=0)
    change = mixed_f - first_f[None]
    main_terms = jnp.sum(second_f[None] * change, axis=1)
    total_terms = jnp.sum(change * change, axis=1)
    return jnp.concatenate([main_terms, total_terms, level_sum[None], square_sum[None]], axis=0)


def indices(sums, base_rows):
    samples = 2.0 * base_rows
    average = sums[2 * P_SIZE] / samples
    variance = sums[2 * P_SIZE + 1] / samples - average * average
    divisor = jnp.maximum(variance, var_floor)
    first_order = sums[:P_SIZE] / base_rows / divisor
    total_order = sums[P_SIZE:2 * P_SIZE] / (2.0 * base_rows) / divisor
    return first_order, total_order, variance


def model_runs(settings, start_field, base_coef, region):
    material = (region[None] == jnp.arange(P_SIZE)[:, None, None]).astype(jnp.float32)
    conduct = base_coef[None] * jnp.einsum("rp,pxy->rxy", settings, material, precision=lax.Precision.HIGHEST)
    widths = ((0, 0), (1, 1), (1, 1))
    padded_coef = jnp.pad(conduct, widths)
    fields_now = jnp.broadcast_to(start_field[None], conduct.shape)
    for section_index in range(STEPS):
        fields_now = diffuse(jnp.pad(fields_now, widths), padded_coef)
    return fields_now


def reference(start_field, base_coef, region, codes_a, codes_b):
    base_rows = codes_a.shape[0]

    def one_row(carry, rows):
        settings = run_params(rows[0], rows[1])
        fields_now = model_runs(settings, start_field, base_coef, region)
        return carry + partial_sums(fields_now[:, None]), None

    initial = jnp.zeros((2 * P_SIZE + 2,) + start_field.shape, jnp.float32)
    sums, unused = lax.scan(one_row, initial, (codes_a, codes_b))
    first_order, total_order, variance = indices(sums, base_rows)
    var_total = jnp.sum(variance)
    aggregate = jnp.stack([jnp.sum(sums[:P_SIZE], axis=(1, 2)) / base_rows / var_total,
                           jnp.sum(sums[P_SIZE:2 * P_SIZE], axis=(1, 2)) / (2.0 * base_rows) / var_total])
    return first_order, total_order, aggregate
```

```python
import functools
import itertools

import jax
import jax.numpy as jnp
import numpy as np
from jax import lax
from jax.experimental import pallas as pl
from jax.experimental.pallas import tpu as pltpu
from jax.sharding import PartitionSpec as P

P_SIZE = 6
STEPS = 3
LANES = 128
KINDS = P_SIZE + 2

code_scale = 1048576.0
lowest = 0.5
spread = 1.9
var_floor = 0.02

CENTER = 1.45
AXES = ("gx", "gy", "sa")

MONO2 = [m for m in itertools.combinations_with_replacement(range(P_SIZE + 1), 2)]
MONO3 = [m for m in itertools.combinations_with_replacement(range(P_SIZE + 1), 3)]
IDX2 = {m: i for i, m in enumerate(MONO2)}
IDX3 = {m: i for i, m in enumerate(MONO3)}
N2 = len(MONO2)
N3 = len(MONO3)
ONE = P_SIZE


def drop(mono, p):
    rest = list(mono)
    rest.remove(p)
    return tuple(rest)


WHOLE = N3 // 16 * 16
LEFT = N3 - WHOLE
SYMBOLS = P_SIZE + 1
CODE_ROW = 3 * STEPS
SEG = 3 * STEPS
TURN = 2 * STEPS


def k_rows():
    rows = [(m, part) for part in range(3) for m in range(WHOLE)]
    rows += [(WHOLE + i, part) for part in range(3) for i in range(LEFT)]
    return rows + [(None, 0)] * (16 - 3 * LEFT)


K_ROWS = k_rows()
K_ALL = len(K_ROWS)


def picks_table():
    table = np.zeros((LANES, 3 * K_ALL), np.float32)
    low = np.zeros((1, K_ALL), np.float32)
    for k, (m, part) in enumerate(K_ROWS):
        if m is None:
            continue
        for f in range(3):
            for piece in range(3):
                table[8 * piece + MONO3[m][f], f * K_ALL + k] = 1.0
        low[0, k] = 1.0 if part == 2 else 0.0
    return table, low


def windows(rows):
    count = -(-rows // (LANES - 2 * STEPS))
    return [
        min(w * (LANES - 2 * STEPS) - STEPS, rows + STEPS - LANES) for w in range(count)
    ]


def sizes(rows):
    nwin = len(windows(rows))
    main = rows + 16
    edge = -(-2 * nwin * SEG // 16) * 16
    return main, main + edge


def places(shape):
    nx, ny, ns = shape
    ix, iy, isa = (lax.axis_index(a) for a in AXES)
    tile = iy * ns + isa
    return {
        "left": jnp.maximum(isa - 1, 0),
        "own": isa,
        "right": jnp.minimum(isa + 1, ns - 1),
        "has_top": ix > 0,
        "has_bot": ix < nx - 1,
        "has_left": tile > 0,
        "has_right": tile < ny * ns - 1,
        "far_left": isa == 0,
        "far_right": isa == ns - 1,
        "first_x": ix == 0,
        "third": isa == 2,
    }


def loop(count, step, fn):
    while count % step:
        step -= 1

    def run(i, carry):
        for k in range(step):
            fn(i * step + k)
        return carry

    lax.fori_loop(0, count // step, run, 0)


def aligned(block):
    return pl.multiple_of(block * 8, 8)


def pack_body(rows, split, shape, *refs):
    f32 = jnp.float32
    fields, (codes_a, codes_b), refs = refs[:3], refs[3:5], refs[5:]
    count = 2 if split else 1
    row_outs, corner_outs, cols_out = refs[:count], refs[count : 2 * count], refs[2 * count]
    upper, lower, tiles_u, tiles_g, upper_g, lower_g, sem = refs[2 * count + 1 :]
    breadth = fields[0].shape[1]
    place = places(shape)
    at = pl.multiple_of(
        jnp.where(place["far_right"], breadth - LANES, 0).astype(jnp.int32), LANES
    )
    copies = []

    def fetch(src, dst):
        copies.append(pltpu.make_async_copy(src, dst, sem.at[len(copies)]))
        copies[-1].start()

    for f in range(3):
        up = upper.at[f] if f < 2 else upper_g
        low = lower.at[f] if f < 2 else lower_g
        tile = tiles_u.at[f] if f < 2 else tiles_g
        fetch(fields[f].at[pl.ds(0, 8), :], up)
        fetch(fields[f].at[pl.ds(rows - 8, 8), :], low)
        fetch(fields[f].at[:, pl.ds(at, LANES)], tile)
    outs = list(row_outs) + list(corner_outs) + [cols_out]
    for out in outs:
        out[CODE_ROW : out.shape[0], :] = jnp.zeros(
            (out.shape[0] - CODE_ROW, out.shape[1]), f32
        )
        n = codes_a.shape[0]
        out[CODE_ROW : CODE_ROW + n, 0:P_SIZE] = codes_a[...].astype(f32)
        out[CODE_ROW + n : CODE_ROW + 2 * n, 0:P_SIZE] = codes_b[...].astype(f32)
    for copy in copies:
        copy.wait()
    for f in range(3):
        up = upper[f] if f < 2 else upper_g[...].astype(f32)
        low = lower[f] if f < 2 else lower_g[...].astype(f32)
        up, low = up[:STEPS], low[8 - STEPS :]
        cut = slice(f * STEPS, (f + 1) * STEPS)
        picked = [low, up] if split else [jnp.where(place["first_x"], low, up)]
        for value, row_out, corner_out in zip(picked, row_outs, corner_outs):
            row_out[cut, :] = value
            corner_out[cut, :] = jnp.where(
                place["third"], value[:, breadth - LANES :], value[:, :LANES]
            )
    lane = lax.broadcasted_iota(jnp.int32, (LANES, LANES), 1)
    turn = jnp.where(place["far_right"], STEPS, 0).astype(jnp.int32)
    for w in range(rows // LANES):
        cut = slice(w * LANES, (w + 1) * LANES)
        wide = None
        for f in range(3):
            tile = tiles_u[f, cut, :] if f < 2 else tiles_g[cut, :].astype(f32)
            moved = pltpu.roll(tile, turn + f * STEPS, 1)
            wide = moved if wide is None else jnp.where(lane >= f * STEPS, moved, wide)
        cols_out[0:CODE_ROW, cut] = wide.T[0:CODE_ROW, :]


def pack(fields, codes_a, codes_b, mesh_shape, split):
    rows, breadth = fields[0].shape
    f32, i32 = jnp.float32, jnp.int32
    height = -(-(CODE_ROW + 2 * codes_a.shape[0]) // 8) * 8
    count = 2 if split else 1
    shapes = [(height, breadth)] * count + [(height, LANES)] * count + [(height, rows)]
    hbm = pl.BlockSpec(memory_space=pl.ANY)
    vmem = pl.BlockSpec(memory_space=pltpu.VMEM)
    return pl.pallas_call(
        functools.partial(pack_body, rows, split, mesh_shape),
        out_shape=tuple(jax.ShapeDtypeStruct(s, f32) for s in shapes),
        in_specs=[hbm] * 3 + [vmem] * 2,
        out_specs=(vmem,) * len(shapes),
        scratch_shapes=[
            pltpu.VMEM((2, 8, breadth), f32),
            pltpu.VMEM((2, 8, breadth), f32),
            pltpu.VMEM((2, rows, LANES), f32),
            pltpu.VMEM((rows, LANES), i32),
            pltpu.VMEM((8, breadth), i32),
            pltpu.VMEM((8, breadth), i32),
            pltpu.SemaphoreType.DMA((9,)),
        ],
        compiler_params=pltpu.CompilerParams(vmem_limit_bytes=56413184),
        name="pack_halo",
    )(*fields, codes_a, codes_b)


def body(
    rows,
    shape,
    u_in,
    k_in,
    g_in,
    top,
    bot,
    ctop,
    cbot,
    cols,
    codes_a,
    codes_b,
    picks,
    lowmask,
    first_out,
    total_out,
    sums_out,
    tile_f,
    tile_g,
    u0,
    be,
    rg,
    mk,
    br,
    bd,
    u1,
    u2,
    fd,
    u3,
    st,
    te,
    et,
    lhs,
    gx,
    cp,
    sset,
    first_v,
    total_v,
    in_sem,
    out_sem,
):
    f32 = jnp.float32
    starts = windows(rows)
    nwin = len(starts)
    main, total = sizes(rows)
    blocks_all = total // 8
    rs3 = u3.shape[0] // (N3 + LEFT)
    rst = st.shape[0] // 17

    place = places(shape)
    has_top, has_bot = place["has_top"], place["has_bot"]
    has_left, has_right = place["has_left"], place["has_right"]
    far_left, far_right = place["far_left"], place["far_right"]
    left_cols, own_cols, right_cols = (
        pl.ds(pl.multiple_of(place[k] * LANES, LANES), LANES) for k in ("left", "own", "right")
    )
    lane8 = lax.broadcasted_iota(jnp.int32, (8, LANES), 1)
    sub8 = lax.broadcasted_iota(jnp.int32, (8, LANES), 0)
    copies = []
    for f, ref in enumerate((u_in, k_in, g_in)):
        for side in (1, 0, 2):
            at = (left_cols, own_cols, right_cols)[side]
            to = tile_f.at[f, side] if f < 2 else tile_g.at[side]
            copy = pltpu.make_async_copy(
                ref.at[:, at], to, in_sem.at[3 * f + side]
            )
            copy.start()
            copies.append(copy)

    per = codes_a.shape[0]
    lam = jnp.zeros((1, K_ALL), f32)
    at = 0
    for src in (None, top, ctop, cols):
        for j in range(per):
            pair = []
            for half, own in enumerate((codes_a, codes_b)):
                if src is None:
                    line = jnp.broadcast_to(own[j : j + 1, :].astype(f32), (8, P_SIZE))
                    pair.append(
                        jnp.concatenate([line, jnp.zeros((8, LANES - P_SIZE), f32)], 1)
                    )
                else:
                    line = CODE_ROW + half * per + j
                    pair.append(src[line : line + 1, 0:LANES])
            a, b = (
                lowest + spread * jnp.broadcast_to(v, (8, LANES)) / code_scale - CENTER
                for v in pair
            )
            v = jnp.where((sub8 == KINDS - 1) | (sub8 == lane8), b, a)
            v = jnp.where(lane8 == ONE, 1.0, v)
            v = jnp.where(lane8 > ONE, 0.0, v)
            hi = v.astype(jnp.bfloat16).astype(f32)
            rest = v - hi
            mid = rest.astype(jnp.bfloat16).astype(f32)
            low = rest - mid
            sset[8 * at : 8 * at + 8, :] = hi + pltpu.roll(mid, 8, 1) + pltpu.roll(low, 16, 1)
            at += 1
    runs = sset.shape[0]
    factors = jnp.dot(
        sset[...].astype(jnp.bfloat16), picks[...], preferred_element_type=f32
    )
    prod = factors[:, :K_ALL] * factors[:, K_ALL : 2 * K_ALL] * factors[:, 2 * K_ALL :]
    sub_k = lax.broadcasted_iota(jnp.int32, (8, K_ALL), 0)
    is_low = jnp.broadcast_to(lowmask[...], (8, K_ALL)) > 0.5

    def put(at, vals):
        hi = vals.astype(jnp.bfloat16).astype(f32)
        lo = (vals - hi).astype(jnp.bfloat16).astype(f32)
        lhs[at : at + 8, :] = jnp.where(is_low, lo, hi)

    for j in range(runs // 8):
        m8 = prod[8 * j : 8 * j + 8, :]
        ma = jnp.broadcast_to(m8[KINDS - 2 : KINDS - 1, :], (8, K_ALL))
        put(8 * j, jnp.where(sub_k < P_SIZE, m8 - ma, m8))
        lam = lam + m8[KINDS - 2 : KINDS - 1, :] + m8[KINDS - 1 : KINDS, :]
    put(runs, jnp.where(sub_k == 0, jnp.broadcast_to(lam, (8, K_ALL)), 0.0))
    lhs_b = lhs[...].astype(jnp.bfloat16)

    zero8 = jnp.zeros((8, LANES), f32)
    for copy in copies:
        copy.wait()

    def tile(f, side, cut):
        return tile_f[f, side, cut, :] if f < 2 else tile_g[side, cut, :].astype(f32)

    row_mask = []
    for ok, edge in ((has_top, 0), (has_bot, 1)):
        near = sub8 >= 8 - STEPS if edge == 0 else sub8 < STEPS
        row_mask.append(jnp.where(near & ok, 1.0, 0.0))
    for f, ref in enumerate((u0, be, rg)):
        scale = 0.5 if f == 1 else 1.0
        cut = slice(f * STEPS, (f + 1) * STEPS)
        ref[0:8, :] = zero8
        ref[main - 8 : main, :] = zero8
        ref[main : ref.shape[0], :] = jnp.zeros((ref.shape[0] - main, LANES), f32)
        ref[8 : 8 + rows, :] = tile(f, 1, slice(None)) * scale
        ref[8 - STEPS : 8, :] = jnp.where(has_top, top[cut, own_cols] * scale, 0.0)
        ref[8 + rows : 8 + rows + STEPS, :] = jnp.where(
            has_bot, bot[cut, own_cols] * scale, 0.0
        )
    mk[0:8, :] = row_mask[0]
    mk[8 : 8 + rows, :] = jnp.ones((rows, LANES), f32)
    mk[8 + rows : main, :] = row_mask[1]
    mk[main : mk.shape[0], :] = jnp.zeros((mk.shape[0] - main, LANES), f32)

    def edges(left, own, right, f):
        lane = lax.broadcasted_iota(jnp.int32, own.shape, 1)
        x = jnp.where(lane >= LANES - STEPS, left, own)
        y = jnp.where(lane < STEPS, right, own)
        x = pltpu.roll(x, 32 * f + STEPS, 1)
        y = pltpu.roll(y, 32 * f + 2 * SEG - STEPS, 1)
        return jnp.where(lane - 32 * f >= SEG, y, x)

    def merge(parts):
        lane = lax.broadcasted_iota(jnp.int32, parts[0].shape, 1)
        v = jnp.where(lane >= 32, parts[1], parts[0])
        return jnp.where(lane >= 64, parts[2], v)

    def gather_edges(block):
        at = aligned(block)
        here = pl.ds(at, 8)
        parts = [edges(tile(f, 0, here), tile(f, 1, here), tile(f, 2, here), f) for f in range(3)]
        gx[pl.ds(pl.multiple_of(at + 8, 8), 8), :] = merge(parts)

    loop(rows // 8, 4, gather_edges)
    for at, near, corner in ((8 - STEPS, top, ctop), (8 + rows, bot, cbot)):
        parts = []
        for f in range(3):
            cut = slice(f * STEPS, (f + 1) * STEPS)
            left = jnp.where(far_left, corner[cut, :], near[cut, left_cols])
            right = jnp.where(far_right, corner[cut, :], near[cut, right_cols])
            parts.append(edges(left, near[cut, own_cols], right, f))
        gx[at : at + STEPS, :] = merge(parts)

    height = cp.shape[0]
    cp[:, 0:LANES] = jnp.zeros((height, LANES), f32)
    cp[:, LANES : LANES + rows] = cols[0:height, :]
    cp[:, LANES + rows : 2 * LANES + rows] = jnp.zeros((height, LANES), f32)
    lane9 = lax.broadcasted_iota(jnp.int32, (SEG, LANES), 1)
    sub9 = lax.broadcasted_iota(jnp.int32, (SEG, LANES), 0)
    for w, start in enumerate(starts):
        turned = gx[start + 8 : start + 8 + LANES, :].T
        far = cp[:, LANES + start : 2 * LANES + start]
        own_row = (lane9 + start >= 0) & (lane9 + start < rows)
        in_rows = ((lane9 + start >= 0) | (has_top)) & (
            (lane9 + start < rows) | (has_bot)
        )
        for side in range(2):
            at = main + SEG * (2 * w + side)
            if side == 0:
                in_cols = (sub9 >= STEPS) | (has_left)
                is_far = (sub9 < STEPS) & own_row & (far_left)
            else:
                in_cols = (sub9 < TURN) | (has_right)
                is_far = (sub9 >= TURN) & own_row & (far_right)
            inside = in_rows & in_cols
            mk[at : at + SEG, :] = inside.astype(f32)
            for f, ref in enumerate((u0, be, rg)):
                v = turned[32 * f + side * SEG : 32 * f + (side + 1) * SEG, :]
                three = far[f * STEPS : (f + 1) * STEPS, :]
                v = jnp.where(is_far, jnp.concatenate([three, three, three], 0), v)
                if f == 1:
                    v = v * 0.5
                if f < 2:
                    v = jnp.where(inside, v, 0.0)
                ref[at : at + SEG, :] = v

    def right_of(v):
        return pltpu.roll(v, LANES - 1, 1)

    def left_of(v):
        return pltpu.roll(v, 1, 1)

    def edge_coefs(block):
        at = aligned(block)
        here, below = pl.ds(at, 8), pl.ds(at + 1, 8)
        b0, r0 = be[here, :], rg[here, :]
        b1, r1 = right_of(b0), right_of(r0)
        b2, r2 = be[below, :], rg[below, :]
        for p in range(P_SIZE):
            own = jnp.where(r0 == p, b0, 0.0)
            br[p, here, :] = own + jnp.where(r1 == p, b1, 0.0)
            bd[p, here, :] = own + jnp.where(r2 == p, b2, 0.0)
        br[ONE, here, :] = CENTER * (b0 + b1)
        bd[ONE, here, :] = CENTER * (b0 + b2)

    loop(blocks_all, 6, edge_coefs)

    def step1(at):
        here, over = pl.ds(at, 8), pl.ds(at - 1, 8)
        c = u0[here, :]
        d_r = right_of(c) - c
        d_d = u0[pl.ds(at + 1, 8), :] - c
        d_u = c - u0[over, :]
        mask8 = mk[here, :]
        for p in range(SYMBOLS):
            f_r = br[p, here, :] * d_r
            v = f_r - left_of(f_r) + (bd[p, here, :] * d_d - bd[p, over, :] * d_u)
            if p == ONE:
                v = v + c
            u1[p, here, :] = v * mask8

    c = u0[0:8, :]
    d_r = right_of(c) - c
    d_d = u0[1:9, :] - c
    for p in range(SYMBOLS):
        f_r = br[p, 0:8, :] * d_r
        f_d = bd[p, 0:8, :] * d_d
        v = f_r - left_of(f_r) + (f_d - pltpu.roll(f_d, 1, 0))
        if p == ONE:
            v = v + c
        u1[p, 0:8, :] = v * mk[0:8, :]
    for p in range(SYMBOLS):
        br[p, total : total + 8, :] = zero8
        bd[p, total : total + 8, :] = zero8
    loop(blocks_all, 6, lambda block: step1(aligned(block + 1)))

    def flux(bs, d, index, mono):
        acc = None
        for p in sorted(set(mono)):
            t = bs[p] * d[index(drop(mono, p))]
            acc = t if acc is None else acc + t
        return acc

    def down(src, index, monos, block):
        at = aligned(block)
        bs = [bd[p, pl.ds(at, 8), :] for p in range(SYMBOLS)]
        count = src.shape[0]
        d = [src[n, pl.ds(at + 1, 8), :] - src[n, pl.ds(at, 8), :] for n in range(count)]
        for n, m in enumerate(monos):
            fd[n, pl.ds(at + 8, 8), :] = flux(bs, d, index, m)

    def across(src, index, monos, emit, block):
        at = aligned(block)
        here = pl.ds(at, 8)
        bs = [br[p, here, :] for p in range(SYMBOLS)]
        d = []
        for n in range(src.shape[0]):
            c = src[n, here, :]
            d.append(right_of(c) - c)
        for n, m in enumerate(monos):
            f_r = flux(bs, d, index, m)
            v = f_r - left_of(f_r)
            v = v + (fd[n, pl.ds(at + 8, 8), :] - fd[n, pl.ds(at + 7, 8), :])
            if m[-1] == ONE:
                v = v + src[index(m[:-1]), here, :]
            emit(n, at, v)

    def index1(m):
        return m[0]

    def index2(m):
        return IDX2[m]

    def put2_masked(n, at, v):
        u2[n, pl.ds(at, 8), :] = v * mk[pl.ds(at, 8), :]

    def put3(n, at, v):
        u3[pl.ds(n * rs3 + at, 8), :] = v

    def put3_twice(n, at, v):
        put3(n, at, v)
        if n >= WHOLE:
            put3(n + LEFT, at, v)

    for n in range(N3):
        fd[n, 0:8, :] = zero8
    for n in range(N2):
        u2[n, total : total + 8, :] = zero8
    def both(src, index, monos, emit, block):
        down(src, index, monos, block)
        across(src, index, monos, emit, block)

    loop(blocks_all, 3, lambda b: down(u1, index1, MONO2, b))
    loop(blocks_all, 3, lambda b: across(u1, index1, MONO2, put2_masked, b))

    keep = 5
    for ref in (br, bd, u2):
        for n in range(ref.shape[0]):
            for k in range(2 * nwin):
                v = ref[n, main + SEG * k + 2 : main + SEG * k + 2 + keep, :]
                ref[n, main + keep * k : main + keep * (k + 1), :] = v
    tail = -(-2 * nwin * keep // 8)
    inner = rows // 8
    outer = main // 8

    def last_blocks(step, fn, first=1):
        loop(inner + 1 - first, step, lambda b: fn(b + first))
        loop(tail, step, lambda b: fn(b + outer))

    down(u2, index2, MONO3, 0)
    last_blocks(1, lambda b: both(u2, index2, MONO3, put3_twice, b))

    first_rows = sub8 < LEFT

    def operand(row):
        hi, lo = [], []
        for g in range(WHOLE // 16):
            v0 = u3[pl.ds(16 * g * rs3 + row, 8, stride=rs3), :]
            v1 = u3[pl.ds((16 * g + 8) * rs3 + row, 8, stride=rs3), :]
            v = jnp.concatenate([v0, v1], 0)
            h = v.astype(jnp.bfloat16)
            hi.append(h)
            lo.append((v - h.astype(f32)).astype(jnp.bfloat16))
        v = u3[pl.ds(WHOLE * rs3 + row, 8, stride=rs3), :]
        h = v.astype(jnp.bfloat16).astype(f32)
        last = jnp.concatenate(
            [jnp.where(first_rows, h, v - h), jnp.where(first_rows, h, 0.0)], 0
        ).astype(jnp.bfloat16)
        return jnp.concatenate(hi + lo + hi + [last], 0)

    def evaluate(row0, row1):
        right = jnp.concatenate([operand(row0), operand(row1)], 1)
        out = jnp.dot(lhs_b, right, preferred_element_type=f32)
        x = out[0:runs].reshape(runs // 8, 8, 2 * LANES)
        y = jnp.broadcast_to(x[:, KINDS - 1 : KINDS, :], x.shape)
        return jnp.sum(x * x, 0), jnp.sum(x * y, 0), out[runs : runs + 1]

    pairs = 8

    def main_pairs(i, carry):
        outs = []
        for k in range(pairs):
            row = i * (2 * pairs) + 2 * k
            outs.append((row, evaluate(row + 8, row + 9)))
        for row, (sq, cr, lv) in outs:
            for h in range(2):
                cut = slice(h * LANES, (h + 1) * LANES)
                st[pl.ds(row + h, 8, stride=rst), :] = sq[:, cut]
                st[pl.ds(8 * rst + row + h, 8, stride=rst), :] = cr[:, cut]
                st[pl.ds(16 * rst + row + h, 1), :] = lv[:, cut]
        return carry

    lax.fori_loop(0, rows // (2 * pairs), main_pairs, 0)

    te[...] = jnp.zeros(te.shape, f32)
    todo = []
    for w in range(nwin):
        for side in range(2):
            for i in range(STEPS):
                at = main + keep * (2 * w + side) + 1 + i
                todo.append((at, w * LANES + (1 - side) * STEPS + i))
    for one, two in zip(todo[0::2], todo[1::2]):
        sq, cr, lv = evaluate(one[0], two[0])
        for h, (_, to) in enumerate((one, two)):
            cut = slice(h * LANES, (h + 1) * LANES)
            te[pl.ds(to, 8, stride=TURN), :] = sq[:, cut]
            te[pl.ds(8 * TURN + to, 8, stride=TURN), :] = cr[:, cut]
            te[pl.ds(16 * TURN + to, 1), :] = lv[:, cut]
    for w, start in enumerate(starts):
        turned = te[w * LANES : (w + 1) * LANES, :].T
        et[start + STEPS : start + LANES - STEPS, :] = turned[STEPS : LANES - STEPS, :]

    is_edge = (lane8 < STEPS) | (lane8 >= LANES - STEPS)
    runs_all = 2.0 * (runs // 8)
    base_rows = runs_all / 2.0
    chunk = 64
    per_chunk = chunk // 8

    def outs(c):
        cut = pl.ds(pl.multiple_of(c * chunk, chunk), chunk)
        return [
            pltpu.make_async_copy(first_v.at[:, cut, :], first_out.at[:, cut, :], out_sem.at[0, c]),
            pltpu.make_async_copy(total_v.at[:, cut, :], total_out.at[:, cut, :], out_sem.at[1, c]),
        ]

    def finish(block, acc):
        at = aligned(block)
        here = pl.ds(at, 8)
        edge = et[here, :]

        def stat(f):
            v = st[pl.ds(pl.multiple_of(f * rst + at, 8), 8), :]
            e = pltpu.roll(edge, (LANES - STEPS - TURN * f) % LANES, 1)
            return jnp.where(is_edge, e, v)

        average = stat(16) / runs_all
        variance = (stat(6) + stat(7)) / runs_all - average * average
        inverse = 1.0 / jnp.maximum(variance, var_floor)
        vals = []
        for p in range(P_SIZE):
            m = stat(8 + p)
            first_v[p, here, :] = m * (1.0 / base_rows) * inverse
            vals.append(m)
        for p in range(P_SIZE):
            t = stat(p)
            total_v[p, here, :] = t * (1.0 / runs_all) * inverse
            vals.append(t)
        vals.append(variance)
        return tuple(a + v for a, v in zip(acc, vals))

    def finish_chunk(c, acc):
        for i in range(per_chunk):
            acc = finish(c * per_chunk + i, acc)
        for copy in outs(c):
            copy.start()
        return acc

    acc = (zero8,) * (2 * P_SIZE + 1)
    acc = lax.fori_loop(0, rows // chunk, finish_chunk, acc)
    lines = [jnp.sum(v, 0, keepdims=True) for v in acc]
    lines = jnp.concatenate(lines + [zero8[0:1]] * (16 - len(lines)), 0)
    each = jnp.broadcast_to(jnp.sum(lines, 1, keepdims=True), (16, LANES))
    lane16 = lax.broadcasted_iota(jnp.int32, (16, LANES), 1)
    sub16 = lax.broadcasted_iota(jnp.int32, (16, LANES), 0)
    line = jnp.sum(jnp.where(lane16 == sub16, each, 0.0), 0, keepdims=True)
    sums_out[...] = jnp.broadcast_to(line, sums_out.shape)
    for c in range(rows // chunk):
        for copy in outs(c):
            copy.wait()


def tile_kernel(mesh_shape, fields, top, bot, ctop, cbot, cols, codes_a, codes_b, devices):
    rows = fields[0].shape[0]
    nwin = len(windows(rows))
    main, total = sizes(rows)
    deep = total + 16
    rs3 = total + 8
    runs = 4 * codes_a.shape[0] * KINDS
    table, low = picks_table()
    f32 = jnp.float32

    hbm = pl.BlockSpec(memory_space=pl.ANY)
    vmem = pl.BlockSpec(memory_space=pltpu.VMEM)
    small = [top, bot, ctop, cbot, cols, codes_a, codes_b]
    small += [jnp.asarray(table, jnp.bfloat16), jnp.asarray(low)]
    outs = (
        jax.ShapeDtypeStruct((P_SIZE, rows, LANES), f32),
        jax.ShapeDtypeStruct((P_SIZE, rows, LANES), f32),
        jax.ShapeDtypeStruct((devices, LANES), f32),
    )
    scratch = [
        pltpu.VMEM((2, 3, rows, LANES), f32),
        pltpu.VMEM((3, rows, LANES), jnp.int32),
        pltpu.VMEM((deep, LANES), f32),
        pltpu.VMEM((deep, LANES), f32),
        pltpu.VMEM((deep, LANES), f32),
        pltpu.VMEM((deep, LANES), f32),
        pltpu.VMEM((SYMBOLS, deep, LANES), f32),
        pltpu.VMEM((SYMBOLS, deep, LANES), f32),
        pltpu.VMEM((SYMBOLS, deep, LANES), f32),
        pltpu.VMEM((N2, deep, LANES), f32),
        pltpu.VMEM((N3, deep, LANES), f32),
        pltpu.VMEM(((N3 + LEFT) * rs3, LANES), f32),
        pltpu.VMEM((17 * rows, LANES), f32),
        pltpu.VMEM((nwin * LANES, LANES), f32),
        pltpu.VMEM((rows, LANES), f32),
        pltpu.VMEM((runs + 8, K_ALL), f32),
        pltpu.VMEM((main, LANES), f32),
        pltpu.VMEM((16, rows + 2 * LANES), f32),
        pltpu.VMEM((runs, LANES), f32),
        pltpu.VMEM((P_SIZE, rows, LANES), f32),
        pltpu.VMEM((P_SIZE, rows, LANES), f32),
        pltpu.SemaphoreType.DMA((9,)),
        pltpu.SemaphoreType.DMA((2, rows // 64)),
    ]
    return pl.pallas_call(
        functools.partial(body, rows, mesh_shape),
        out_shape=outs,
        in_specs=[hbm] * 3 + [vmem] * len(small),
        out_specs=(hbm, hbm, vmem),
        scratch_shapes=scratch,
        compiler_params=pltpu.CompilerParams(vmem_limit_bytes=52 * 2**20),
        name="sobol_tile",
    )(*fields, *small)


def ratio_body(base_rows, parts, out):
    grand = jnp.sum(parts[...], 0, keepdims=True)
    lane = lax.broadcasted_iota(jnp.int32, grand.shape, 1)
    var_total = jnp.sum(jnp.where(lane == 2 * P_SIZE, grand, 0.0), 1, keepdims=True)
    first = grand[:, 0:P_SIZE] / base_rows / var_total
    total = pltpu.roll(grand, LANES - P_SIZE, 1)[:, 0:P_SIZE] / (2.0 * base_rows) / var_total
    out[0:1, :] = first
    out[1:2, :] = total


def local(start_field, base_coef, region, codes_a, codes_b):
    rows, breadth = start_field.shape
    nx, ny, ns = (lax.axis_size(a) for a in AXES)
    if ns != 4 or breadth != ns * LANES or rows % LANES:
        raise ValueError("unsupported mesh")
    devices = nx * ny * ns

    def permute(value, dx, dy, flip):
        pairs = []
        for x, y, s in itertools.product(range(nx), range(ny), range(ns)):
            sy = y
            if dy:
                sy = (y - 1) % ny if s == 0 else (y + 1) % ny if s == ns - 1 else y
            src = (((x + dx) % nx) * ny + sy) * ns + (s ^ flip)
            pairs.append((src, (x * ny + y) * ns + s))
        return lax.ppermute(value, AXES, pairs)

    fields = (start_field, base_coef, region)
    split = nx > 2
    mesh_shape = (nx, ny, ns)
    sent = pack(fields, codes_a, codes_b, mesh_shape, split)
    if split:
        top = permute(sent[0], -1, False, 1)
        bot = permute(sent[1], 1, False, 1)
        ctop = permute(sent[2], -1, True, 2)
        cbot = permute(sent[3], 1, True, 2)
    else:
        top = bot = permute(sent[0], nx - 1, False, 1)
        ctop = cbot = permute(sent[1], nx - 1, True, 2)
    cols = permute(sent[-1], 0, True, 3)
    first_order, total_order, sums = tile_kernel(
        mesh_shape, fields, top, bot, ctop, cbot, cols, codes_a, codes_b, devices
    )
    parts = lax.all_to_all(sums, AXES, 0, 0, tiled=True)
    aggregate = pl.pallas_call(
        functools.partial(ratio_body, ns * codes_a.shape[0]),
        out_shape=jax.ShapeDtypeStruct((2, P_SIZE), jnp.float32),
        in_specs=[pl.BlockSpec(memory_space=pltpu.VMEM)],
        out_specs=pl.BlockSpec(memory_space=pltpu.VMEM),
        compiler_params=pltpu.CompilerParams(vmem_limit_bytes=2**20),
        name="ratios",
    )(parts)
    return first_order, total_order, aggregate


def solution(mesh):
    placed = (P("gx", "gy"), P("gx", "gy"), P("gx", "gy"), P("sa", None), P("sa", None))
    return jax.shard_map(
        local,
        mesh=mesh,
        in_specs=placed,
        out_specs=(P(None, "gx", ("gy", "sa")), P(None, "gx", ("gy", "sa")), P()),
        check_vma=False,
    )
```

```python
import functools
import itertools

import jax
import jax.numpy as jnp
import numpy as np
from jax import lax
from jax.experimental import pallas as pl
from jax.experimental.pallas import tpu as pltpu
from jax.sharding import PartitionSpec as P

P_SIZE = 6
STEPS = 3
LANES = 128
KINDS = P_SIZE + 2

code_scale = 1048576.0
lowest = 0.5
spread = 1.9
var_floor = 0.02

CENTER = 1.45
AXES = ("gx", "gy", "sa")

MONO2 = [m for m in itertools.combinations_with_replacement(range(P_SIZE + 1), 2)]
MONO3 = [m for m in itertools.combinations_with_replacement(range(P_SIZE + 1), 3)]
IDX2 = {m: i for i, m in enumerate(MONO2)}
IDX3 = {m: i for i, m in enumerate(MONO3)}
N2 = len(MONO2)
N3 = len(MONO3)
ONE = P_SIZE


def drop(mono, p):
    rest = list(mono)
    rest.remove(p)
    return tuple(rest)


WHOLE = N3 // 16 * 16
LEFT = N3 - WHOLE
SYMBOLS = P_SIZE + 1
CODE_ROW = 3 * STEPS
SEG = 3 * STEPS
TURN = 2 * STEPS


def k_rows():
    rows = [(m, part) for part in range(3) for m in range(WHOLE)]
    rows += [(WHOLE + i, part) for part in range(3) for i in range(LEFT)]
    return rows + [(None, 0)] * (16 - 3 * LEFT)


K_ROWS = k_rows()
K_ALL = len(K_ROWS)


def stairs(at, values):
    out = jnp.full(at.shape, values[0], jnp.int32)
    for i in range(1, len(values)):
        if values[i] != values[i - 1]:
            out = out + jnp.where(at >= i, values[i] - values[i - 1], 0)
    return out


def picks_table():
    column = lax.broadcasted_iota(jnp.int32, (8, K_ALL), 1)
    mono = stairs(column, [0 if m is None else m - k for k, (m, _) in enumerate(K_ROWS)])
    mono = mono + column
    used = column < 3 * N3
    sub = lax.broadcasted_iota(jnp.int32, (8, K_ALL), 0)
    tables = []
    for f in range(3):
        slope = 1 if f == 2 else 0
        symbol = stairs(mono, [m[f] - slope * n for n, m in enumerate(MONO3)]) + slope * mono
        one = jnp.where((symbol == sub) & used, 1.0, 0.0)
        tables.append(jnp.concatenate([one, one, one, jnp.zeros((8, K_ALL), jnp.float32)], 0))
    low = (column >= 2 * WHOLE) & (column < 3 * WHOLE)
    low = low | ((column >= 3 * WHOLE + 2 * LEFT) & used)
    return jnp.concatenate(tables, 1).astype(jnp.bfloat16), low


def windows(rows):
    count = -(-rows // (LANES - 2 * STEPS))
    return [
        min(w * (LANES - 2 * STEPS) - STEPS, rows + STEPS - LANES) for w in range(count)
    ]


def sizes(rows):
    nwin = len(windows(rows))
    main = rows + 16
    edge = -(-2 * nwin * SEG // 16) * 16
    return main, main + edge


def places(shape):
    nx, ny, ns = shape
    ix, iy, isa = (lax.axis_index(a) for a in AXES)
    tile = iy * ns + isa
    return {
        "left": jnp.maximum(isa - 1, 0),
        "own": isa,
        "right": jnp.minimum(isa + 1, ns - 1),
        "has_top": ix > 0,
        "has_bot": ix < nx - 1,
        "has_left": tile > 0,
        "has_right": tile < ny * ns - 1,
        "far_left": isa == 0,
        "far_right": isa == ns - 1,
        "first_x": ix == 0,
        "third": isa == 2,
    }


def loop(count, step, fn):
    while count % step:
        step -= 1

    def run(i, carry):
        for k in range(step):
            fn(i * step + k)
        return carry

    lax.fori_loop(0, count // step, run, 0)


def aligned(block):
    return pl.multiple_of(block * 8, 8)


def pack_body(rows, split, shape, *refs):
    f32 = jnp.float32
    fields, (codes_a, codes_b), refs = refs[:3], refs[3:5], refs[5:]
    count = 2 if split else 1
    row_outs, corner_outs, cols_out = refs[:count], refs[count : 2 * count], refs[2 * count]
    upper, lower, tiles_u, tiles_g, upper_g, lower_g, sem = refs[2 * count + 1 :]
    breadth = fields[0].shape[1]
    place = places(shape)
    at = pl.multiple_of(
        jnp.where(place["far_right"], breadth - LANES, 0).astype(jnp.int32), LANES
    )
    copies = []

    def fetch(src, dst):
        copies.append(pltpu.make_async_copy(src, dst, sem.at[len(copies)]))
        copies[-1].start()

    for f in range(3):
        up = upper.at[f] if f < 2 else upper_g
        low = lower.at[f] if f < 2 else lower_g
        tile = tiles_u.at[f] if f < 2 else tiles_g
        fetch(fields[f].at[pl.ds(0, 8), :], up)
        fetch(fields[f].at[pl.ds(rows - 8, 8), :], low)
        fetch(fields[f].at[:, pl.ds(at, LANES)], tile)
    outs = list(row_outs) + list(corner_outs) + [cols_out]
    for out in outs:
        out[CODE_ROW : out.shape[0], :] = jnp.zeros(
            (out.shape[0] - CODE_ROW, out.shape[1]), f32
        )
        n = codes_a.shape[0]
        out[CODE_ROW : CODE_ROW + n, 0:P_SIZE] = codes_a[...].astype(f32)
        out[CODE_ROW + n : CODE_ROW + 2 * n, 0:P_SIZE] = codes_b[...].astype(f32)
    for copy in copies:
        copy.wait()
    for f in range(3):
        up = upper[f] if f < 2 else upper_g[...].astype(f32)
        low = lower[f] if f < 2 else lower_g[...].astype(f32)
        up, low = up[:STEPS], low[8 - STEPS :]
        cut = slice(f * STEPS, (f + 1) * STEPS)
        picked = [low, up] if split else [jnp.where(place["first_x"], low, up)]
        for value, row_out, corner_out in zip(picked, row_outs, corner_outs):
            row_out[cut, :] = value
            corner_out[cut, :] = jnp.where(
                place["third"], value[:, breadth - LANES :], value[:, :LANES]
            )
    lane = lax.broadcasted_iota(jnp.int32, (LANES, LANES), 1)
    turn = jnp.where(place["far_right"], STEPS, 0).astype(jnp.int32)
    for w in range(rows // LANES):
        cut = slice(w * LANES, (w + 1) * LANES)
        wide = None
        for f in range(3):
            tile = tiles_u[f, cut, :] if f < 2 else tiles_g[cut, :].astype(f32)
            moved = pltpu.roll(tile, turn + f * STEPS, 1)
            wide = moved if wide is None else jnp.where(lane >= f * STEPS, moved, wide)
        cols_out[0:CODE_ROW, cut] = wide.T[0:CODE_ROW, :]


def pack(fields, codes_a, codes_b, mesh_shape, split):
    rows, breadth = fields[0].shape
    f32, i32 = jnp.float32, jnp.int32
    height = -(-(CODE_ROW + 2 * codes_a.shape[0]) // 8) * 8
    count = 2 if split else 1
    shapes = [(height, breadth)] * count + [(height, LANES)] * count + [(height, rows)]
    hbm = pl.BlockSpec(memory_space=pl.ANY)
    vmem = pl.BlockSpec(memory_space=pltpu.VMEM)
    return pl.pallas_call(
        functools.partial(pack_body, rows, split, mesh_shape),
        out_shape=tuple(jax.ShapeDtypeStruct(s, f32) for s in shapes),
        in_specs=[hbm] * 3 + [vmem] * 2,
        out_specs=(vmem,) * len(shapes),
        scratch_shapes=[
            pltpu.VMEM((2, 8, breadth), f32),
            pltpu.VMEM((2, 8, breadth), f32),
            pltpu.VMEM((2, rows, LANES), f32),
            pltpu.VMEM((rows, LANES), i32),
            pltpu.VMEM((8, breadth), i32),
            pltpu.VMEM((8, breadth), i32),
            pltpu.SemaphoreType.DMA((9,)),
        ],
        compiler_params=pltpu.CompilerParams(vmem_limit_bytes=56413184),
        name="pack_halo",
    )(*fields, codes_a, codes_b)


def body(
    rows,
    shape,
    u_in,
    k_in,
    g_in,
    top,
    bot,
    ctop,
    cbot,
    cols,
    own_codes,
    first_out,
    total_out,
    sums_out,
    tile_f,
    tile_g,
    u0,
    be,
    rg,
    mk,
    br,
    bd,
    u1,
    u2,
    fd,
    u3,
    st,
    te,
    et,
    lhs,
    gx,
    cp,
    sset,
    first_v,
    total_v,
    in_sem,
    out_sem,
):
    f32 = jnp.float32
    starts = windows(rows)
    nwin = len(starts)
    main, total = sizes(rows)
    blocks_all = total // 8
    rs3 = u3.shape[0] // (N3 + LEFT)
    rst = st.shape[0] // 17

    place = places(shape)
    has_top, has_bot = place["has_top"], place["has_bot"]
    has_left, has_right = place["has_left"], place["has_right"]
    far_left, far_right = place["far_left"], place["far_right"]
    left_cols, own_cols, right_cols = (
        pl.ds(pl.multiple_of(place[k] * LANES, LANES), LANES) for k in ("left", "own", "right")
    )
    lane8 = lax.broadcasted_iota(jnp.int32, (8, LANES), 1)
    sub8 = lax.broadcasted_iota(jnp.int32, (8, LANES), 0)
    copies = []
    for f, ref in enumerate((u_in, k_in, g_in)):
        for side in (1, 0, 2):
            at = (left_cols, own_cols, right_cols)[side]
            to = tile_f.at[f, side] if f < 2 else tile_g.at[side]
            copy = pltpu.make_async_copy(
                ref.at[:, at], to, in_sem.at[3 * f + side]
            )
            copy.start()
            copies.append(copy)

    per = sset.shape[0] // (4 * KINDS)
    lam = jnp.zeros((1, K_ALL), f32)
    at = 0
    for src in (own_codes, top, ctop, cols):
        for j in range(per):
            pair = []
            for half in range(2):
                line = CODE_ROW + half * per + j
                pair.append(src[line : line + 1, 0:LANES])
            a, b = (
                lowest + spread * jnp.broadcast_to(v, (8, LANES)) / code_scale - CENTER
                for v in pair
            )
            v = jnp.where((sub8 == KINDS - 1) | (sub8 == lane8), b, a)
            v = jnp.where(lane8 == ONE, 1.0, v)
            v = jnp.where(lane8 > ONE, 0.0, v)
            hi = v.astype(jnp.bfloat16).astype(f32)
            rest = v - hi
            mid = rest.astype(jnp.bfloat16).astype(f32)
            low = rest - mid
            sset[8 * at : 8 * at + 8, :] = hi + pltpu.roll(mid, 8, 1) + pltpu.roll(low, 16, 1)
            at += 1
    runs = sset.shape[0]
    picks, is_low = picks_table()
    factors = jnp.dot(
        sset[:, 0 : picks.shape[0]].astype(jnp.bfloat16), picks, preferred_element_type=f32
    )
    prod = factors[:, :K_ALL] * factors[:, K_ALL : 2 * K_ALL] * factors[:, 2 * K_ALL :]
    sub_k = lax.broadcasted_iota(jnp.int32, (8, K_ALL), 0)

    def put(at, vals):
        hi = vals.astype(jnp.bfloat16).astype(f32)
        lo = (vals - hi).astype(jnp.bfloat16).astype(f32)
        lhs[at : at + 8, :] = jnp.where(is_low, lo, hi)

    for j in range(runs // 8):
        m8 = prod[8 * j : 8 * j + 8, :]
        ma = jnp.broadcast_to(m8[KINDS - 2 : KINDS - 1, :], (8, K_ALL))
        put(8 * j, jnp.where(sub_k < P_SIZE, m8 - ma, m8))
        lam = lam + m8[KINDS - 2 : KINDS - 1, :] + m8[KINDS - 1 : KINDS, :]
    put(runs, jnp.where(sub_k == 0, jnp.broadcast_to(lam, (8, K_ALL)), 0.0))
    lhs_b = lhs[...].astype(jnp.bfloat16)

    zero8 = jnp.zeros((8, LANES), f32)
    for copy in copies:
        copy.wait()

    def tile(f, side, cut):
        return tile_f[f, side, cut, :] if f < 2 else tile_g[side, cut, :].astype(f32)

    row_mask = []
    for ok, edge in ((has_top, 0), (has_bot, 1)):
        near = sub8 >= 8 - STEPS if edge == 0 else sub8 < STEPS
        row_mask.append(jnp.where(near & ok, 1.0, 0.0))
    for f, ref in enumerate((u0, be, rg)):
        scale = 0.5 if f == 1 else 1.0
        cut = slice(f * STEPS, (f + 1) * STEPS)
        ref[0:8, :] = zero8
        ref[main - 8 : main, :] = zero8
        ref[main : ref.shape[0], :] = jnp.zeros((ref.shape[0] - main, LANES), f32)
        ref[8 : 8 + rows, :] = tile(f, 1, slice(None)) * scale
        ref[8 - STEPS : 8, :] = jnp.where(has_top, top[cut, own_cols] * scale, 0.0)
        ref[8 + rows : 8 + rows + STEPS, :] = jnp.where(
            has_bot, bot[cut, own_cols] * scale, 0.0
        )
    mk[0:8, :] = row_mask[0]
    mk[8 : 8 + rows, :] = jnp.ones((rows, LANES), f32)
    mk[8 + rows : main, :] = row_mask[1]
    mk[main : mk.shape[0], :] = jnp.zeros((mk.shape[0] - main, LANES), f32)

    def edges(left, own, right, f):
        lane = lax.broadcasted_iota(jnp.int32, own.shape, 1)
        x = jnp.where(lane >= LANES - STEPS, left, own)
        y = jnp.where(lane < STEPS, right, own)
        x = pltpu.roll(x, 32 * f + STEPS, 1)
        y = pltpu.roll(y, 32 * f + 2 * SEG - STEPS, 1)
        return jnp.where(lane - 32 * f >= SEG, y, x)

    def merge(parts):
        lane = lax.broadcasted_iota(jnp.int32, parts[0].shape, 1)
        v = jnp.where(lane >= 32, parts[1], parts[0])
        return jnp.where(lane >= 64, parts[2], v)

    def gather_edges(block):
        at = aligned(block)
        here = pl.ds(at, 8)
        parts = [edges(tile(f, 0, here), tile(f, 1, here), tile(f, 2, here), f) for f in range(3)]
        gx[pl.ds(pl.multiple_of(at + 8, 8), 8), :] = merge(parts)

    loop(rows // 8, 4, gather_edges)
    for at, near, corner in ((8 - STEPS, top, ctop), (8 + rows, bot, cbot)):
        parts = []
        for f in range(3):
            cut = slice(f * STEPS, (f + 1) * STEPS)
            left = jnp.where(far_left, corner[cut, :], near[cut, left_cols])
            right = jnp.where(far_right, corner[cut, :], near[cut, right_cols])
            parts.append(edges(left, near[cut, own_cols], right, f))
        gx[at : at + STEPS, :] = merge(parts)

    height = cp.shape[0]
    cp[:, 0:LANES] = jnp.zeros((height, LANES), f32)
    cp[:, LANES : LANES + rows] = cols[0:height, :]
    cp[:, LANES + rows : 2 * LANES + rows] = jnp.zeros((height, LANES), f32)
    lane9 = lax.broadcasted_iota(jnp.int32, (SEG, LANES), 1)
    sub9 = lax.broadcasted_iota(jnp.int32, (SEG, LANES), 0)
    for w, start in enumerate(starts):
        turned = gx[start + 8 : start + 8 + LANES, :].T
        far = cp[:, LANES + start : 2 * LANES + start]
        own_row = (lane9 + start >= 0) & (lane9 + start < rows)
        in_rows = ((lane9 + start >= 0) | (has_top)) & (
            (lane9 + start < rows) | (has_bot)
        )
        for side in range(2):
            at = main + SEG * (2 * w + side)
            if side == 0:
                in_cols = (sub9 >= STEPS) | (has_left)
                is_far = (sub9 < STEPS) & own_row & (far_left)
            else:
                in_cols = (sub9 < TURN) | (has_right)
                is_far = (sub9 >= TURN) & own_row & (far_right)
            inside = in_rows & in_cols
            mk[at : at + SEG, :] = inside.astype(f32)
            for f, ref in enumerate((u0, be, rg)):
                v = turned[32 * f + side * SEG : 32 * f + (side + 1) * SEG, :]
                three = far[f * STEPS : (f + 1) * STEPS, :]
                v = jnp.where(is_far, jnp.concatenate([three, three, three], 0), v)
                if f == 1:
                    v = v * 0.5
                if f < 2:
                    v = jnp.where(inside, v, 0.0)
                ref[at : at + SEG, :] = v

    def right_of(v):
        return pltpu.roll(v, LANES - 1, 1)

    def left_of(v):
        return pltpu.roll(v, 1, 1)

    def edge_coefs(block):
        at = aligned(block)
        here, below = pl.ds(at, 8), pl.ds(at + 1, 8)
        b0, r0 = be[here, :], rg[here, :]
        b1, r1 = right_of(b0), right_of(r0)
        b2, r2 = be[below, :], rg[below, :]
        for p in range(P_SIZE):
            own = jnp.where(r0 == p, b0, 0.0)
            br[p, here, :] = own + jnp.where(r1 == p, b1, 0.0)
            bd[p, here, :] = own + jnp.where(r2 == p, b2, 0.0)
        br[ONE, here, :] = CENTER * (b0 + b1)
        bd[ONE, here, :] = CENTER * (b0 + b2)

    loop(blocks_all, 6, edge_coefs)

    def step1(at):
        here, over = pl.ds(at, 8), pl.ds(at - 1, 8)
        c = u0[here, :]
        d_r = right_of(c) - c
        d_d = u0[pl.ds(at + 1, 8), :] - c
        d_u = c - u0[over, :]
        mask8 = mk[here, :]
        for p in range(SYMBOLS):
            f_r = br[p, here, :] * d_r
            v = f_r - left_of(f_r) + (bd[p, here, :] * d_d - bd[p, over, :] * d_u)
            if p == ONE:
                v = v + c
            u1[p, here, :] = v * mask8

    c = u0[0:8, :]
    d_r = right_of(c) - c
    d_d = u0[1:9, :] - c
    for p in range(SYMBOLS):
        f_r = br[p, 0:8, :] * d_r
        f_d = bd[p, 0:8, :] * d_d
        v = f_r - left_of(f_r) + (f_d - pltpu.roll(f_d, 1, 0))
        if p == ONE:
            v = v + c
        u1[p, 0:8, :] = v * mk[0:8, :]
    for p in range(SYMBOLS):
        br[p, total : total + 8, :] = zero8
        bd[p, total : total + 8, :] = zero8
    loop(blocks_all, 6, lambda block: step1(aligned(block + 1)))

    def flux(bs, d, index, mono):
        acc = None
        for p in sorted(set(mono)):
            t = bs[p] * d[index(drop(mono, p))]
            acc = t if acc is None else acc + t
        return acc

    def down(src, index, monos, block):
        at = aligned(block)
        bs = [bd[p, pl.ds(at, 8), :] for p in range(SYMBOLS)]
        count = src.shape[0]
        d = [src[n, pl.ds(at + 1, 8), :] - src[n, pl.ds(at, 8), :] for n in range(count)]
        for n, m in enumerate(monos):
            fd[n, pl.ds(at + 8, 8), :] = flux(bs, d, index, m)

    def across(src, index, monos, emit, block):
        at = aligned(block)
        here = pl.ds(at, 8)
        bs = [br[p, here, :] for p in range(SYMBOLS)]
        d = []
        for n in range(src.shape[0]):
            c = src[n, here, :]
            d.append(right_of(c) - c)
        for n, m in enumerate(monos):
            f_r = flux(bs, d, index, m)
            v = f_r - left_of(f_r)
            v = v + (fd[n, pl.ds(at + 8, 8), :] - fd[n, pl.ds(at + 7, 8), :])
            if m[-1] == ONE:
                v = v + src[index(m[:-1]), here, :]
            emit(n, at, v)

    def index1(m):
        return m[0]

    def index2(m):
        return IDX2[m]

    def put2_masked(n, at, v):
        u2[n, pl.ds(at, 8), :] = v * mk[pl.ds(at, 8), :]

    def put3(n, at, v):
        u3[pl.ds(n * rs3 + at, 8), :] = v

    def put3_twice(n, at, v):
        put3(n, at, v)
        if n >= WHOLE:
            put3(n + LEFT, at, v)

    for n in range(N3):
        fd[n, 0:8, :] = zero8
    for n in range(N2):
        u2[n, total : total + 8, :] = zero8
    def both(src, index, monos, emit, block):
        down(src, index, monos, block)
        across(src, index, monos, emit, block)

    loop(blocks_all, 3, lambda b: down(u1, index1, MONO2, b))
    loop(blocks_all, 3, lambda b: across(u1, index1, MONO2, put2_masked, b))

    keep = 5
    for ref in (br, bd, u2):
        for n in range(ref.shape[0]):
            for k in range(2 * nwin):
                v = ref[n, main + SEG * k + 2 : main + SEG * k + 2 + keep, :]
                ref[n, main + keep * k : main + keep * (k + 1), :] = v
    tail = -(-2 * nwin * keep // 8)
    inner = rows // 8
    outer = main // 8

    def last_blocks(step, fn, first=1):
        loop(inner + 1 - first, step, lambda b: fn(b + first))
        loop(tail, step, lambda b: fn(b + outer))

    down(u2, index2, MONO3, 0)
    last_blocks(1, lambda b: both(u2, index2, MONO3, put3_twice, b))

    first_rows = sub8 < LEFT

    def operand(row):
        hi, lo = [], []
        for g in range(WHOLE // 16):
            v0 = u3[pl.ds(16 * g * rs3 + row, 8, stride=rs3), :]
            v1 = u3[pl.ds((16 * g + 8) * rs3 + row, 8, stride=rs3), :]
            v = jnp.concatenate([v0, v1], 0)
            h = v.astype(jnp.bfloat16)
            hi.append(h)
            lo.append((v - h.astype(f32)).astype(jnp.bfloat16))
        v = u3[pl.ds(WHOLE * rs3 + row, 8, stride=rs3), :]
        h = v.astype(jnp.bfloat16).astype(f32)
        last = jnp.concatenate(
            [jnp.where(first_rows, h, v - h), jnp.where(first_rows, h, 0.0)], 0
        ).astype(jnp.bfloat16)
        return jnp.concatenate(hi + lo + hi + [last], 0)

    def evaluate(row0, row1):
        right = jnp.concatenate([operand(row0), operand(row1)], 1)
        out = jnp.dot(lhs_b, right, preferred_element_type=f32)
        x = out[0:runs].reshape(runs // 8, 8, 2 * LANES)
        y = jnp.broadcast_to(x[:, KINDS - 1 : KINDS, :], x.shape)
        return jnp.sum(x * x, 0), jnp.sum(x * y, 0), out[runs : runs + 1]

    pairs = 8

    def main_pairs(i, carry):
        outs = []
        for k in range(pairs):
            row = i * (2 * pairs) + 2 * k
            outs.append((row, evaluate(row + 8, row + 9)))
        for row, (sq, cr, lv) in outs:
            for h in range(2):
                cut = slice(h * LANES, (h + 1) * LANES)
                st[pl.ds(row + h, 8, stride=rst), :] = sq[:, cut]
                st[pl.ds(8 * rst + row + h, 8, stride=rst), :] = cr[:, cut]
                st[pl.ds(16 * rst + row + h, 1), :] = lv[:, cut]
        return carry

    lax.fori_loop(0, rows // (2 * pairs), main_pairs, 0)

    te[...] = jnp.zeros(te.shape, f32)
    todo = []
    for w in range(nwin):
        for side in range(2):
            for i in range(STEPS):
                at = main + keep * (2 * w + side) + 1 + i
                todo.append((at, w * LANES + (1 - side) * STEPS + i))
    for one, two in zip(todo[0::2], todo[1::2]):
        sq, cr, lv = evaluate(one[0], two[0])
        for h, (_, to) in enumerate((one, two)):
            cut = slice(h * LANES, (h + 1) * LANES)
            te[pl.ds(to, 8, stride=TURN), :] = sq[:, cut]
            te[pl.ds(8 * TURN + to, 8, stride=TURN), :] = cr[:, cut]
            te[pl.ds(16 * TURN + to, 1), :] = lv[:, cut]
    for w, start in enumerate(starts):
        turned = te[w * LANES : (w + 1) * LANES, :].T
        et[start + STEPS : start + LANES - STEPS, :] = turned[STEPS : LANES - STEPS, :]

    is_edge = (lane8 < STEPS) | (lane8 >= LANES - STEPS)
    runs_all = 2.0 * (runs // 8)
    base_rows = runs_all / 2.0
    chunk = 64
    per_chunk = chunk // 8

    def outs(c):
        cut = pl.ds(pl.multiple_of(c * chunk, chunk), chunk)
        return [
            pltpu.make_async_copy(first_v.at[:, cut, :], first_out.at[:, cut, :], out_sem.at[0, c]),
            pltpu.make_async_copy(total_v.at[:, cut, :], total_out.at[:, cut, :], out_sem.at[1, c]),
        ]

    def finish(block, acc):
        at = aligned(block)
        here = pl.ds(at, 8)
        edge = et[here, :]

        def stat(f):
            v = st[pl.ds(pl.multiple_of(f * rst + at, 8), 8), :]
            e = pltpu.roll(edge, (LANES - STEPS - TURN * f) % LANES, 1)
            return jnp.where(is_edge, e, v)

        average = stat(16) / runs_all
        variance = (stat(6) + stat(7)) / runs_all - average * average
        inverse = 1.0 / jnp.maximum(variance, var_floor)
        vals = []
        for p in range(P_SIZE):
            m = stat(8 + p)
            first_v[p, here, :] = m * (1.0 / base_rows) * inverse
            vals.append(m)
        for p in range(P_SIZE):
            t = stat(p)
            total_v[p, here, :] = t * (1.0 / runs_all) * inverse
            vals.append(t)
        vals.append(variance)
        return tuple(a + v for a, v in zip(acc, vals))

    def finish_chunk(c, acc):
        for i in range(per_chunk):
            acc = finish(c * per_chunk + i, acc)
        for copy in outs(c):
            copy.start()
        return acc

    acc = (zero8,) * (2 * P_SIZE + 1)
    acc = lax.fori_loop(0, rows // chunk, finish_chunk, acc)
    lines = [jnp.sum(v, 0, keepdims=True) for v in acc]
    lines = jnp.concatenate(lines + [zero8[0:1]] * (16 - len(lines)), 0)
    each = jnp.broadcast_to(jnp.sum(lines, 1, keepdims=True), (16, LANES))
    lane16 = lax.broadcasted_iota(jnp.int32, (16, LANES), 1)
    sub16 = lax.broadcasted_iota(jnp.int32, (16, LANES), 0)
    line = jnp.sum(jnp.where(lane16 == sub16, each, 0.0), 0, keepdims=True)
    sums_out[...] = jnp.broadcast_to(line, sums_out.shape)
    for c in range(rows // chunk):
        for copy in outs(c):
            copy.wait()


def tile_kernel(mesh_shape, fields, small, base_rows, devices):
    rows = fields[0].shape[0]
    nwin = len(windows(rows))
    main, total = sizes(rows)
    deep = total + 16
    rs3 = total + 8
    runs = base_rows * KINDS
    f32 = jnp.float32

    hbm = pl.BlockSpec(memory_space=pl.ANY)
    vmem = pl.BlockSpec(memory_space=pltpu.VMEM)
    outs = (
        jax.ShapeDtypeStruct((P_SIZE, rows, LANES), f32),
        jax.ShapeDtypeStruct((P_SIZE, rows, LANES), f32),
        jax.ShapeDtypeStruct((devices, LANES), f32),
    )
    scratch = [
        pltpu.VMEM((2, 3, rows, LANES), f32),
        pltpu.VMEM((3, rows, LANES), jnp.int32),
        pltpu.VMEM((deep, LANES), f32),
        pltpu.VMEM((deep, LANES), f32),
        pltpu.VMEM((deep, LANES), f32),
        pltpu.VMEM((deep, LANES), f32),
        pltpu.VMEM((SYMBOLS, deep, LANES), f32),
        pltpu.VMEM((SYMBOLS, deep, LANES), f32),
        pltpu.VMEM((SYMBOLS, deep, LANES), f32),
        pltpu.VMEM((N2, deep, LANES), f32),
        pltpu.VMEM((N3, deep, LANES), f32),
        pltpu.VMEM(((N3 + LEFT) * rs3, LANES), f32),
        pltpu.VMEM((17 * rows, LANES), f32),
        pltpu.VMEM((nwin * LANES, LANES), f32),
        pltpu.VMEM((rows, LANES), f32),
        pltpu.VMEM((runs + 8, K_ALL), f32),
        pltpu.VMEM((main, LANES), f32),
        pltpu.VMEM((16, rows + 2 * LANES), f32),
        pltpu.VMEM((runs, LANES), f32),
        pltpu.VMEM((P_SIZE, rows, LANES), f32),
        pltpu.VMEM((P_SIZE, rows, LANES), f32),
        pltpu.SemaphoreType.DMA((9,)),
        pltpu.SemaphoreType.DMA((2, rows // 64)),
    ]
    return pl.pallas_call(
        functools.partial(body, rows, mesh_shape),
        out_shape=outs,
        in_specs=[hbm] * 3 + [vmem] * len(small),
        out_specs=(hbm, hbm, vmem),
        scratch_shapes=scratch,
        compiler_params=pltpu.CompilerParams(
            vmem_limit_bytes=52 * 2**20,
        ),
        name="sobol_tile",
    )(*fields, *small)


def ratio_body(base_rows, parts, out):
    grand = jnp.sum(parts[...], 0, keepdims=True)
    lane = lax.broadcasted_iota(jnp.int32, grand.shape, 1)
    var_total = jnp.sum(jnp.where(lane == 2 * P_SIZE, grand, 0.0), 1, keepdims=True)
    first = grand[:, 0:P_SIZE] / base_rows / var_total
    total = pltpu.roll(grand, LANES - P_SIZE, 1)[:, 0:P_SIZE] / (2.0 * base_rows) / var_total
    out[0:1, :] = first
    out[1:2, :] = total


def local(start_field, base_coef, region, codes_a, codes_b):
    rows, breadth = start_field.shape
    nx, ny, ns = (lax.axis_size(a) for a in AXES)
    if ns != 4 or breadth != ns * LANES or rows % LANES:
        raise ValueError("unsupported mesh")
    devices = nx * ny * ns

    def permute(value, dx, dy, flip):
        pairs = []
        for x, y, s in itertools.product(range(nx), range(ny), range(ns)):
            sy = y
            if dy:
                sy = (y - 1) % ny if s == 0 else (y + 1) % ny if s == ns - 1 else y
            src = (((x + dx) % nx) * ny + sy) * ns + (s ^ flip)
            pairs.append((src, (x * ny + y) * ns + s))
        return lax.ppermute(value, AXES, pairs)

    fields = (start_field, base_coef, region)
    split = nx > 2
    mesh_shape = (nx, ny, ns)
    sent = pack(fields, codes_a, codes_b, mesh_shape, split)
    if split:
        top = permute(sent[0], -1, False, 1)
        bot = permute(sent[1], 1, False, 1)
        ctop = permute(sent[2], -1, True, 2)
        cbot = permute(sent[3], 1, True, 2)
    else:
        top = bot = permute(sent[0], nx - 1, False, 1)
        ctop = cbot = permute(sent[1], nx - 1, True, 2)
    cols = permute(sent[-1], 0, True, 3)
    small = [top, bot, ctop, cbot, cols, sent[-2]]
    first_order, total_order, sums = tile_kernel(
        mesh_shape, fields, small, ns * codes_a.shape[0], devices
    )
    parts = lax.all_to_all(sums, AXES, 0, 0, tiled=True)
    aggregate = pl.pallas_call(
        functools.partial(ratio_body, ns * codes_a.shape[0]),
        out_shape=jax.ShapeDtypeStruct((2, P_SIZE), jnp.float32),
        in_specs=[pl.BlockSpec(memory_space=pltpu.VMEM)],
        out_specs=pl.BlockSpec(memory_space=pltpu.VMEM),
        compiler_params=pltpu.CompilerParams(vmem_limit_bytes=2**20),
        name="ratios",
    )(parts)
    return first_order, total_order, aggregate


def solution(mesh):
    placed = (P("gx", "gy"), P("gx", "gy"), P("gx", "gy"), P("sa", None), P("sa", None))
    return jax.shard_map(
        local,
        mesh=mesh,
        in_specs=placed,
        out_specs=(P(None, "gx", ("gy", "sa")), P(None, "gx", ("gy", "sa")), P()),
        check_vma=False,
    )
```

```python
import functools
import itertools

import jax
import jax.numpy as jnp
import numpy as np
from jax import lax
from jax.experimental import pallas as pl
from jax.experimental.pallas import tpu as pltpu
from jax.sharding import PartitionSpec as P

P_SIZE = 6
STEPS = 3
LANES = 128
KINDS = P_SIZE + 2

code_scale = 1048576.0
lowest = 0.5
spread = 1.9
var_floor = 0.02

CENTER = 1.45
AXES = ("gx", "gy", "sa")

MONO2 = [m for m in itertools.combinations_with_replacement(range(P_SIZE + 1), 2)]
MONO3 = [m for m in itertools.combinations_with_replacement(range(P_SIZE + 1), 3)]
IDX2 = {m: i for i, m in enumerate(MONO2)}
IDX3 = {m: i for i, m in enumerate(MONO3)}
N2 = len(MONO2)
N3 = len(MONO3)
ONE = P_SIZE


def drop(mono, p):
    rest = list(mono)
    rest.remove(p)
    return tuple(rest)


WHOLE = N3 // 16 * 16
LEFT = N3 - WHOLE
SYMBOLS = P_SIZE + 1
CODE_ROW = 3 * STEPS
SEG = 3 * STEPS
TURN = 2 * STEPS


def k_rows():
    rows = [(m, part) for part in range(3) for m in range(WHOLE)]
    rows += [(WHOLE + i, part) for part in range(3) for i in range(LEFT)]
    return rows + [(None, 0)] * (16 - 3 * LEFT)


K_ROWS = k_rows()
K_ALL = len(K_ROWS)


def stairs(at, values):
    out = jnp.full(at.shape, values[0], jnp.int32)
    for i in range(1, len(values)):
        if values[i] != values[i - 1]:
            out = out + jnp.where(at >= i, values[i] - values[i - 1], 0)
    return out


def picks_table():
    column = lax.broadcasted_iota(jnp.int32, (8, K_ALL), 1)
    mono = stairs(column, [0 if m is None else m - k for k, (m, _) in enumerate(K_ROWS)])
    mono = mono + column
    used = column < 3 * N3
    sub = lax.broadcasted_iota(jnp.int32, (8, K_ALL), 0)
    tables = []
    for f in range(3):
        slope = 1 if f == 2 else 0
        symbol = stairs(mono, [m[f] - slope * n for n, m in enumerate(MONO3)]) + slope * mono
        one = jnp.where((symbol == sub) & used, 1.0, 0.0)
        tables.append(jnp.concatenate([one, one, one, jnp.zeros((8, K_ALL), jnp.float32)], 0))
    low = (column >= 2 * WHOLE) & (column < 3 * WHOLE)
    low = low | ((column >= 3 * WHOLE + 2 * LEFT) & used)
    return jnp.concatenate(tables, 1).astype(jnp.bfloat16), low


def windows(rows):
    count = -(-rows // (LANES - 2 * STEPS))
    return [
        min(w * (LANES - 2 * STEPS) - STEPS, rows + STEPS - LANES) for w in range(count)
    ]


def sizes(rows):
    nwin = len(windows(rows))
    main = rows + 16
    edge = -(-2 * nwin * SEG // 16) * 16
    return main, main + edge


def places(shape):
    nx, ny, ns = shape
    ix, iy, isa = (lax.axis_index(a) for a in AXES)
    tile = iy * ns + isa
    return {
        "left": jnp.maximum(isa - 1, 0),
        "own": isa,
        "right": jnp.minimum(isa + 1, ns - 1),
        "has_top": ix > 0,
        "has_bot": ix < nx - 1,
        "has_left": tile > 0,
        "has_right": tile < ny * ns - 1,
        "far_left": isa == 0,
        "far_right": isa == ns - 1,
        "first_x": ix == 0,
        "third": isa == 2,
    }


def loop(count, step, fn):
    while count % step:
        step -= 1

    def run(i, carry):
        for k in range(step):
            fn(i * step + k)
        return carry

    lax.fori_loop(0, count // step, run, 0)


def aligned(block):
    return pl.multiple_of(block * 8, 8)


def pack_body(rows, split, shape, *refs):
    f32 = jnp.float32
    fields, (codes_a, codes_b), refs = refs[:3], refs[3:5], refs[5:]
    count = 2 if split else 1
    row_outs, corner_outs, cols_out = refs[:count], refs[count : 2 * count], refs[2 * count]
    upper, lower, tiles_u, tiles_g, upper_g, lower_g, sem = refs[2 * count + 1 :]
    breadth = fields[0].shape[1]
    place = places(shape)
    at = pl.multiple_of(
        jnp.where(place["far_right"], breadth - LANES, 0).astype(jnp.int32), LANES
    )
    copies = []

    def fetch(src, dst):
        copies.append(pltpu.make_async_copy(src, dst, sem.at[len(copies)]))
        copies[-1].start()

    for f in range(3):
        up = upper.at[f] if f < 2 else upper_g
        low = lower.at[f] if f < 2 else lower_g
        tile = tiles_u.at[f] if f < 2 else tiles_g
        fetch(fields[f].at[pl.ds(0, 8), :], up)
        fetch(fields[f].at[pl.ds(rows - 8, 8), :], low)
        fetch(fields[f].at[:, pl.ds(at, LANES)], tile)
    outs = list(row_outs) + list(corner_outs) + [cols_out]
    for out in outs:
        out[CODE_ROW : out.shape[0], :] = jnp.zeros(
            (out.shape[0] - CODE_ROW, out.shape[1]), f32
        )
        n = codes_a.shape[0]
        out[CODE_ROW : CODE_ROW + n, 0:P_SIZE] = codes_a[...].astype(f32)
        out[CODE_ROW + n : CODE_ROW + 2 * n, 0:P_SIZE] = codes_b[...].astype(f32)
    for copy in copies:
        copy.wait()
    for f in range(3):
        up = upper[f] if f < 2 else upper_g[...].astype(f32)
        low = lower[f] if f < 2 else lower_g[...].astype(f32)
        up, low = up[:STEPS], low[8 - STEPS :]
        cut = slice(f * STEPS, (f + 1) * STEPS)
        picked = [low, up] if split else [jnp.where(place["first_x"], low, up)]
        for value, row_out, corner_out in zip(picked, row_outs, corner_outs):
            row_out[cut, :] = value
            corner_out[cut, :] = jnp.where(
                place["third"], value[:, breadth - LANES :], value[:, :LANES]
            )
    lane = lax.broadcasted_iota(jnp.int32, (LANES, LANES), 1)
    turn = jnp.where(place["far_right"], STEPS, 0).astype(jnp.int32)
    for w in range(rows // LANES):
        cut = slice(w * LANES, (w + 1) * LANES)
        wide = None
        for f in range(3):
            tile = tiles_u[f, cut, :] if f < 2 else tiles_g[cut, :].astype(f32)
            moved = pltpu.roll(tile, turn + f * STEPS, 1)
            wide = moved if wide is None else jnp.where(lane >= f * STEPS, moved, wide)
        cols_out[0:CODE_ROW, cut] = wide.T[0:CODE_ROW, :]


def pack(fields, codes_a, codes_b, mesh_shape, split):
    rows, breadth = fields[0].shape
    f32, i32 = jnp.float32, jnp.int32
    height = -(-(CODE_ROW + 2 * codes_a.shape[0]) // 8) * 8
    count = 2 if split else 1
    shapes = [(height, breadth)] * count + [(height, LANES)] * count + [(height, rows)]
    hbm = pl.BlockSpec(memory_space=pl.ANY)
    vmem = pl.BlockSpec(memory_space=pltpu.VMEM)
    return pl.pallas_call(
        functools.partial(pack_body, rows, split, mesh_shape),
        out_shape=tuple(jax.ShapeDtypeStruct(s, f32) for s in shapes),
        in_specs=[hbm] * 3 + [vmem] * 2,
        out_specs=(vmem,) * len(shapes),
        scratch_shapes=[
            pltpu.VMEM((2, 8, breadth), f32),
            pltpu.VMEM((2, 8, breadth), f32),
            pltpu.VMEM((2, rows, LANES), f32),
            pltpu.VMEM((rows, LANES), i32),
            pltpu.VMEM((8, breadth), i32),
            pltpu.VMEM((8, breadth), i32),
            pltpu.SemaphoreType.DMA((9,)),
        ],
        compiler_params=pltpu.CompilerParams(vmem_limit_bytes=56413184),
        name="pack_halo",
    )(*fields, codes_a, codes_b)


def body(
    rows,
    shape,
    u_in,
    k_in,
    g_in,
    top,
    bot,
    ctop,
    cbot,
    cols,
    own_codes,
    first_out,
    total_out,
    sums_out,
    tile_f,
    tile_g,
    u0,
    be,
    rg,
    mk,
    br,
    bd,
    u1,
    u2,
    fd,
    u3,
    st,
    te,
    et,
    lhs,
    gx,
    cp,
    sset,
    first_v,
    total_v,
    in_sem,
    out_sem,
):
    f32 = jnp.float32
    starts = windows(rows)
    nwin = len(starts)
    main, total = sizes(rows)
    blocks_all = total // 8
    rs3 = u3.shape[0] // (N3 + LEFT)
    rst = st.shape[0] // 17

    place = places(shape)
    has_top, has_bot = place["has_top"], place["has_bot"]
    has_left, has_right = place["has_left"], place["has_right"]
    far_left, far_right = place["far_left"], place["far_right"]
    left_cols, own_cols, right_cols = (
        pl.ds(pl.multiple_of(place[k] * LANES, LANES), LANES) for k in ("left", "own", "right")
    )
    lane8 = lax.broadcasted_iota(jnp.int32, (8, LANES), 1)
    sub8 = lax.broadcasted_iota(jnp.int32, (8, LANES), 0)
    copies = []
    for f, ref in enumerate((u_in, k_in, g_in)):
        for side in (1, 0, 2):
            at = (left_cols, own_cols, right_cols)[side]
            to = tile_f.at[f, side] if f < 2 else tile_g.at[side]
            copy = pltpu.make_async_copy(
                ref.at[:, at], to, in_sem.at[3 * f + side]
            )
            copy.start()
            copies.append(copy)

    per = sset.shape[0] // (4 * KINDS)
    lam = jnp.zeros((1, K_ALL), f32)
    at = 0
    for src in (own_codes, top, ctop, cols):
        for j in range(per):
            pair = []
            for half in range(2):
                line = CODE_ROW + half * per + j
                pair.append(src[line : line + 1, 0:LANES])
            a, b = (
                lowest + spread * jnp.broadcast_to(v, (8, LANES)) / code_scale - CENTER
                for v in pair
            )
            v = jnp.where((sub8 == KINDS - 1) | (sub8 == lane8), b, a)
            v = jnp.where(lane8 == ONE, 1.0, v)
            v = jnp.where(lane8 > ONE, 0.0, v)
            hi = v.astype(jnp.bfloat16).astype(f32)
            rest = v - hi
            mid = rest.astype(jnp.bfloat16).astype(f32)
            low = rest - mid
            sset[8 * at : 8 * at + 8, :] = hi + pltpu.roll(mid, 8, 1) + pltpu.roll(low, 16, 1)
            at += 1
    runs = sset.shape[0]
    picks, is_low = picks_table()
    factors = jnp.dot(
        sset[:, 0 : picks.shape[0]].astype(jnp.bfloat16), picks, preferred_element_type=f32
    )
    prod = factors[:, :K_ALL] * factors[:, K_ALL : 2 * K_ALL] * factors[:, 2 * K_ALL :]
    sub_k = lax.broadcasted_iota(jnp.int32, (8, K_ALL), 0)

    def put(at, vals):
        hi = vals.astype(jnp.bfloat16).astype(f32)
        lo = (vals - hi).astype(jnp.bfloat16).astype(f32)
        lhs[at : at + 8, :] = jnp.where(is_low, lo, hi)

    for j in range(runs // 8):
        m8 = prod[8 * j : 8 * j + 8, :]
        ma = jnp.broadcast_to(m8[KINDS - 2 : KINDS - 1, :], (8, K_ALL))
        put(8 * j, jnp.where(sub_k < P_SIZE, m8 - ma, m8))
        lam = lam + m8[KINDS - 2 : KINDS - 1, :] + m8[KINDS - 1 : KINDS, :]
    put(runs, jnp.where(sub_k == 0, jnp.broadcast_to(lam, (8, K_ALL)), 0.0))
    lhs_b = lhs[...].astype(jnp.bfloat16)

    zero8 = jnp.zeros((8, LANES), f32)
    for copy in copies:
        copy.wait()

    def tile(f, side, cut):
        return tile_f[f, side, cut, :] if f < 2 else tile_g[side, cut, :].astype(f32)

    row_mask = []
    for ok, edge in ((has_top, 0), (has_bot, 1)):
        near = sub8 >= 8 - STEPS if edge == 0 else sub8 < STEPS
        row_mask.append(jnp.where(near & ok, 1.0, 0.0))
    for f, ref in enumerate((u0, be, rg)):
        scale = 0.5 if f == 1 else 1.0
        cut = slice(f * STEPS, (f + 1) * STEPS)
        ref[0:8, :] = zero8
        ref[main - 8 : main, :] = zero8
        ref[main : ref.shape[0], :] = jnp.zeros((ref.shape[0] - main, LANES), f32)
        ref[8 : 8 + rows, :] = tile(f, 1, slice(None)) * scale
        ref[8 - STEPS : 8, :] = jnp.where(has_top, top[cut, own_cols] * scale, 0.0)
        ref[8 + rows : 8 + rows + STEPS, :] = jnp.where(
            has_bot, bot[cut, own_cols] * scale, 0.0
        )
    mk[0:8, :] = row_mask[0]
    mk[8 : 8 + rows, :] = jnp.ones((rows, LANES), f32)
    mk[8 + rows : main, :] = row_mask[1]
    mk[main : mk.shape[0], :] = jnp.zeros((mk.shape[0] - main, LANES), f32)

    def edges(left, own, right, f):
        lane = lax.broadcasted_iota(jnp.int32, own.shape, 1)
        x = jnp.where(lane >= LANES - STEPS, left, own)
        y = jnp.where(lane < STEPS, right, own)
        x = pltpu.roll(x, 32 * f + STEPS, 1)
        y = pltpu.roll(y, 32 * f + 2 * SEG - STEPS, 1)
        return jnp.where(lane - 32 * f >= SEG, y, x)

    def merge(parts):
        lane = lax.broadcasted_iota(jnp.int32, parts[0].shape, 1)
        v = jnp.where(lane >= 32, parts[1], parts[0])
        return jnp.where(lane >= 64, parts[2], v)

    def gather_edges(block):
        at = aligned(block)
        here = pl.ds(at, 8)
        parts = [edges(tile(f, 0, here), tile(f, 1, here), tile(f, 2, here), f) for f in range(3)]
        gx[pl.ds(pl.multiple_of(at + 8, 8), 8), :] = merge(parts)

    loop(rows // 8, 4, gather_edges)
    for at, near, corner in ((8 - STEPS, top, ctop), (8 + rows, bot, cbot)):
        parts = []
        for f in range(3):
            cut = slice(f * STEPS, (f + 1) * STEPS)
            left = jnp.where(far_left, corner[cut, :], near[cut, left_cols])
            right = jnp.where(far_right, corner[cut, :], near[cut, right_cols])
            parts.append(edges(left, near[cut, own_cols], right, f))
        gx[at : at + STEPS, :] = merge(parts)

    height = cp.shape[0]
    cp[:, 0:LANES] = jnp.zeros((height, LANES), f32)
    cp[:, LANES : LANES + rows] = cols[0:height, :]
    cp[:, LANES + rows : 2 * LANES + rows] = jnp.zeros((height, LANES), f32)
    lane9 = lax.broadcasted_iota(jnp.int32, (SEG, LANES), 1)
    sub9 = lax.broadcasted_iota(jnp.int32, (SEG, LANES), 0)
    for w, start in enumerate(starts):
        turned = gx[start + 8 : start + 8 + LANES, :].T
        far = cp[:, LANES + start : 2 * LANES + start]
        own_row = (lane9 + start >= 0) & (lane9 + start < rows)
        in_rows = ((lane9 + start >= 0) | (has_top)) & (
            (lane9 + start < rows) | (has_bot)
        )
        for side in range(2):
            at = main + SEG * (2 * w + side)
            if side == 0:
                in_cols = (sub9 >= STEPS) | (has_left)
                is_far = (sub9 < STEPS) & own_row & (far_left)
            else:
                in_cols = (sub9 < TURN) | (has_right)
                is_far = (sub9 >= TURN) & own_row & (far_right)
            inside = in_rows & in_cols
            mk[at : at + SEG, :] = inside.astype(f32)
            for f, ref in enumerate((u0, be, rg)):
                v = turned[32 * f + side * SEG : 32 * f + (side + 1) * SEG, :]
                three = far[f * STEPS : (f + 1) * STEPS, :]
                v = jnp.where(is_far, jnp.concatenate([three, three, three], 0), v)
                if f == 1:
                    v = v * 0.5
                if f < 2:
                    v = jnp.where(inside, v, 0.0)
                ref[at : at + SEG, :] = v

    def right_of(v):
        return pltpu.roll(v, LANES - 1, 1)

    def left_of(v):
        return pltpu.roll(v, 1, 1)

    def edge_coefs(block):
        at = aligned(block)
        here, below = pl.ds(at, 8), pl.ds(at + 1, 8)
        b0, r0 = be[here, :], rg[here, :]
        b1, r1 = right_of(b0), right_of(r0)
        b2, r2 = be[below, :], rg[below, :]
        for p in range(P_SIZE):
            own = jnp.where(r0 == p, b0, 0.0)
            br[p, here, :] = own + jnp.where(r1 == p, b1, 0.0)
            bd[p, here, :] = own + jnp.where(r2 == p, b2, 0.0)
        br[ONE, here, :] = CENTER * (b0 + b1)
        bd[ONE, here, :] = CENTER * (b0 + b2)

    loop(blocks_all, 6, edge_coefs)

    def step1(at):
        here, over = pl.ds(at, 8), pl.ds(at - 1, 8)
        c = u0[here, :]
        d_r = right_of(c) - c
        d_d = u0[pl.ds(at + 1, 8), :] - c
        d_u = c - u0[over, :]
        mask8 = mk[here, :]
        for p in range(SYMBOLS):
            f_r = br[p, here, :] * d_r
            v = f_r - left_of(f_r) + (bd[p, here, :] * d_d - bd[p, over, :] * d_u)
            if p == ONE:
                v = v + c
            u1[p, here, :] = v * mask8

    c = u0[0:8, :]
    d_r = right_of(c) - c
    d_d = u0[1:9, :] - c
    for p in range(SYMBOLS):
        f_r = br[p, 0:8, :] * d_r
        f_d = bd[p, 0:8, :] * d_d
        v = f_r - left_of(f_r) + (f_d - pltpu.roll(f_d, 1, 0))
        if p == ONE:
            v = v + c
        u1[p, 0:8, :] = v * mk[0:8, :]
    for p in range(SYMBOLS):
        br[p, total : total + 8, :] = zero8
        bd[p, total : total + 8, :] = zero8
    loop(blocks_all, 6, lambda block: step1(aligned(block + 1)))

    def flux(bs, d, index, mono):
        acc = None
        for p in sorted(set(mono)):
            t = bs[p] * d[index(drop(mono, p))]
            acc = t if acc is None else acc + t
        return acc

    def down(src, index, monos, block):
        at = aligned(block)
        bs = [bd[p, pl.ds(at, 8), :] for p in range(SYMBOLS)]
        count = src.shape[0]
        d = [src[n, pl.ds(at + 1, 8), :] - src[n, pl.ds(at, 8), :] for n in range(count)]
        for n, m in enumerate(monos):
            fd[n, pl.ds(at + 8, 8), :] = flux(bs, d, index, m)

    def across(src, index, monos, emit, block):
        at = aligned(block)
        here = pl.ds(at, 8)
        bs = [br[p, here, :] for p in range(SYMBOLS)]
        d = []
        for n in range(src.shape[0]):
            c = src[n, here, :]
            d.append(right_of(c) - c)
        for n, m in enumerate(monos):
            f_r = flux(bs, d, index, m)
            v = f_r - left_of(f_r)
            v = v + (fd[n, pl.ds(at + 8, 8), :] - fd[n, pl.ds(at + 7, 8), :])
            if m[-1] == ONE:
                v = v + src[index(m[:-1]), here, :]
            emit(n, at, v)

    def index1(m):
        return m[0]

    def index2(m):
        return IDX2[m]

    def put2_masked(n, at, v):
        u2[n, pl.ds(at, 8), :] = v * mk[pl.ds(at, 8), :]

    def put3(n, at, v):
        u3[pl.ds(n * rs3 + at, 8), :] = v

    def put3_twice(n, at, v):
        put3(n, at, v)
        if n >= WHOLE:
            put3(n + LEFT, at, v)

    for n in range(N3):
        fd[n, 0:8, :] = zero8
    for n in range(N2):
        u2[n, total : total + 8, :] = zero8
    def both(src, index, monos, emit, block):
        down(src, index, monos, block)
        across(src, index, monos, emit, block)

    loop(blocks_all, 3, lambda b: down(u1, index1, MONO2, b))
    loop(blocks_all, 3, lambda b: across(u1, index1, MONO2, put2_masked, b))

    keep = 5
    for ref in (br, bd, u2):
        for n in range(ref.shape[0]):
            for k in range(2 * nwin):
                v = ref[n, main + SEG * k + 2 : main + SEG * k + 2 + keep, :]
                ref[n, main + keep * k : main + keep * (k + 1), :] = v
    tail = -(-2 * nwin * keep // 8)
    outer = main // 8

    down(u2, index2, MONO3, 0)
    loop(tail, 1, lambda b: both(u2, index2, MONO3, put3_twice, b + outer))

    first_rows = sub8 < LEFT

    def operand(row):
        hi, lo = [], []
        for g in range(WHOLE // 16):
            v0 = u3[pl.ds(16 * g * rs3 + row, 8, stride=rs3), :]
            v1 = u3[pl.ds((16 * g + 8) * rs3 + row, 8, stride=rs3), :]
            v = jnp.concatenate([v0, v1], 0)
            h = v.astype(jnp.bfloat16)
            hi.append(h)
            lo.append((v - h.astype(f32)).astype(jnp.bfloat16))
        v = u3[pl.ds(WHOLE * rs3 + row, 8, stride=rs3), :]
        h = v.astype(jnp.bfloat16).astype(f32)
        last = jnp.concatenate(
            [jnp.where(first_rows, h, v - h), jnp.where(first_rows, h, 0.0)], 0
        ).astype(jnp.bfloat16)
        return jnp.concatenate(hi + lo + hi + [last], 0)

    def evaluate(row0, row1):
        right = jnp.concatenate([operand(row0), operand(row1)], 1)
        out = jnp.dot(lhs_b, right, preferred_element_type=f32)
        x = out[0:runs].reshape(runs // 8, 8, 2 * LANES)
        y = jnp.broadcast_to(x[:, KINDS - 1 : KINDS, :], x.shape)
        return jnp.sum(x * x, 0), jnp.sum(x * y, 0), out[runs : runs + 1]

    pairs = 8

    def main_pairs(i, carry):
        outs = []
        for k in range(pairs):
            row = i * (2 * pairs) + 2 * k
            outs.append((row, evaluate(row + 8, row + 9)))
        for row, (sq, cr, lv) in outs:
            for h in range(2):
                cut = slice(h * LANES, (h + 1) * LANES)
                st[pl.ds(row + h, 8, stride=rst), :] = sq[:, cut]
                st[pl.ds(8 * rst + row + h, 8, stride=rst), :] = cr[:, cut]
                st[pl.ds(16 * rst + row + h, 1), :] = lv[:, cut]
        return carry

    def both3(block):
        both(u2, index2, MONO3, put3_twice, block)

    per_turn = 2 * pairs // 8

    def turn(i, carry):
        main_pairs(i - 1, 0)
        for k in range(per_turn):
            both3(i * per_turn + 1 + k)
        return carry

    for k in range(per_turn):
        both3(1 + k)
    turns = rows // (2 * pairs)
    lax.fori_loop(1, turns, turn, 0)
    main_pairs(turns - 1, 0)

    te[...] = jnp.zeros(te.shape, f32)
    todo = []
    for w in range(nwin):
        for side in range(2):
            for i in range(STEPS):
                at = main + keep * (2 * w + side) + 1 + i
                todo.append((at, w * LANES + (1 - side) * STEPS + i))
    for one, two in zip(todo[0::2], todo[1::2]):
        sq, cr, lv = evaluate(one[0], two[0])
        for h, (_, to) in enumerate((one, two)):
            cut = slice(h * LANES, (h + 1) * LANES)
            te[pl.ds(to, 8, stride=TURN), :] = sq[:, cut]
            te[pl.ds(8 * TURN + to, 8, stride=TURN), :] = cr[:, cut]
            te[pl.ds(16 * TURN + to, 1), :] = lv[:, cut]
    for w, start in enumerate(starts):
        turned = te[w * LANES : (w + 1) * LANES, :].T
        et[start + STEPS : start + LANES - STEPS, :] = turned[STEPS : LANES - STEPS, :]

    is_edge = (lane8 < STEPS) | (lane8 >= LANES - STEPS)
    runs_all = 2.0 * (runs // 8)
    base_rows = runs_all / 2.0
    chunk = 64
    per_chunk = chunk // 8

    def outs(c):
        cut = pl.ds(pl.multiple_of(c * chunk, chunk), chunk)
        return [
            pltpu.make_async_copy(first_v.at[:, cut, :], first_out.at[:, cut, :], out_sem.at[0, c]),
            pltpu.make_async_copy(total_v.at[:, cut, :], total_out.at[:, cut, :], out_sem.at[1, c]),
        ]

    def finish(block, acc):
        at = aligned(block)
        here = pl.ds(at, 8)
        edge = et[here, :]

        def stat(f):
            v = st[pl.ds(pl.multiple_of(f * rst + at, 8), 8), :]
            e = pltpu.roll(edge, (LANES - STEPS - TURN * f) % LANES, 1)
            return jnp.where(is_edge, e, v)

        average = stat(16) / runs_all
        variance = (stat(6) + stat(7)) / runs_all - average * average
        inverse = 1.0 / jnp.maximum(variance, var_floor)
        vals = []
        for p in range(P_SIZE):
            m = stat(8 + p)
            first_v[p, here, :] = m * (1.0 / base_rows) * inverse
            vals.append(m)
        for p in range(P_SIZE):
            t = stat(p)
            total_v[p, here, :] = t * (1.0 / runs_all) * inverse
            vals.append(t)
        vals.append(variance)
        return tuple(a + v for a, v in zip(acc, vals))

    def finish_chunk(c, acc):
        for i in range(per_chunk):
            acc = finish(c * per_chunk + i, acc)
        for copy in outs(c):
            copy.start()
        return acc

    acc = (zero8,) * (2 * P_SIZE + 1)
    acc = lax.fori_loop(0, rows // chunk, finish_chunk, acc)
    lines = [jnp.sum(v, 0, keepdims=True) for v in acc]
    lines = jnp.concatenate(lines + [zero8[0:1]] * (16 - len(lines)), 0)
    each = jnp.broadcast_to(jnp.sum(lines, 1, keepdims=True), (16, LANES))
    lane16 = lax.broadcasted_iota(jnp.int32, (16, LANES), 1)
    sub16 = lax.broadcasted_iota(jnp.int32, (16, LANES), 0)
    line = jnp.sum(jnp.where(lane16 == sub16, each, 0.0), 0, keepdims=True)
    sums_out[...] = jnp.broadcast_to(line, sums_out.shape)
    for c in range(rows // chunk):
        for copy in outs(c):
            copy.wait()


def tile_kernel(mesh_shape, fields, small, base_rows, devices):
    rows = fields[0].shape[0]
    nwin = len(windows(rows))
    main, total = sizes(rows)
    deep = total + 16
    rs3 = total + 8
    runs = base_rows * KINDS
    f32 = jnp.float32

    hbm = pl.BlockSpec(memory_space=pl.ANY)
    vmem = pl.BlockSpec(memory_space=pltpu.VMEM)
    outs = (
        jax.ShapeDtypeStruct((P_SIZE, rows, LANES), f32),
        jax.ShapeDtypeStruct((P_SIZE, rows, LANES), f32),
        jax.ShapeDtypeStruct((devices, LANES), f32),
    )
    scratch = [
        pltpu.VMEM((2, 3, rows, LANES), f32),
        pltpu.VMEM((3, rows, LANES), jnp.int32),
        pltpu.VMEM((deep, LANES), f32),
        pltpu.VMEM((deep, LANES), f32),
        pltpu.VMEM((deep, LANES), f32),
        pltpu.VMEM((deep, LANES), f32),
        pltpu.VMEM((SYMBOLS, deep, LANES), f32),
        pltpu.VMEM((SYMBOLS, deep, LANES), f32),
        pltpu.VMEM((SYMBOLS, deep, LANES), f32),
        pltpu.VMEM((N2, deep, LANES), f32),
        pltpu.VMEM((N3, deep, LANES), f32),
        pltpu.VMEM(((N3 + LEFT) * rs3, LANES), f32),
        pltpu.VMEM((17 * rows, LANES), f32),
        pltpu.VMEM((nwin * LANES, LANES), f32),
        pltpu.VMEM((rows, LANES), f32),
        pltpu.VMEM((runs + 8, K_ALL), f32),
        pltpu.VMEM((main, LANES), f32),
        pltpu.VMEM((16, rows + 2 * LANES), f32),
        pltpu.VMEM((runs, LANES), f32),
        pltpu.VMEM((P_SIZE, rows, LANES), f32),
        pltpu.VMEM((P_SIZE, rows, LANES), f32),
        pltpu.SemaphoreType.DMA((9,)),
        pltpu.SemaphoreType.DMA((2, rows // 64)),
    ]
    return pl.pallas_call(
        functools.partial(body, rows, mesh_shape),
        out_shape=outs,
        in_specs=[hbm] * 3 + [vmem] * len(small),
        out_specs=(hbm, hbm, vmem),
        scratch_shapes=scratch,
        compiler_params=pltpu.CompilerParams(
            vmem_limit_bytes=52 * 2**20,
        ),
        name="sobol_tile",
    )(*fields, *small)


def ratio_body(base_rows, parts, out):
    grand = jnp.sum(parts[...], 0, keepdims=True)
    lane = lax.broadcasted_iota(jnp.int32, grand.shape, 1)
    var_total = jnp.sum(jnp.where(lane == 2 * P_SIZE, grand, 0.0), 1, keepdims=True)
    first = grand[:, 0:P_SIZE] / base_rows / var_total
    total = pltpu.roll(grand, LANES - P_SIZE, 1)[:, 0:P_SIZE] / (2.0 * base_rows) / var_total
    out[0:1, :] = first
    out[1:2, :] = total


def local(start_field, base_coef, region, codes_a, codes_b):
    rows, breadth = start_field.shape
    nx, ny, ns = (lax.axis_size(a) for a in AXES)
    if ns != 4 or breadth != ns * LANES or rows % LANES:
        raise ValueError("unsupported mesh")
    devices = nx * ny * ns

    def permute(value, dx, dy, flip):
        pairs = []
        for x, y, s in itertools.product(range(nx), range(ny), range(ns)):
            sy = y
            if dy:
                sy = (y - 1) % ny if s == 0 else (y + 1) % ny if s == ns - 1 else y
            src = (((x + dx) % nx) * ny + sy) * ns + (s ^ flip)
            pairs.append((src, (x * ny + y) * ns + s))
        return lax.ppermute(value, AXES, pairs)

    fields = (start_field, base_coef, region)
    split = nx > 2
    mesh_shape = (nx, ny, ns)
    sent = pack(fields, codes_a, codes_b, mesh_shape, split)
    if split:
        top = permute(sent[0], -1, False, 1)
        bot = permute(sent[1], 1, False, 1)
        ctop = permute(sent[2], -1, True, 2)
        cbot = permute(sent[3], 1, True, 2)
    else:
        top = bot = permute(sent[0], nx - 1, False, 1)
        ctop = cbot = permute(sent[1], nx - 1, True, 2)
    cols = permute(sent[-1], 0, True, 3)
    small = [top, bot, ctop, cbot, cols, sent[-2]]
    first_order, total_order, sums = tile_kernel(
        mesh_shape, fields, small, ns * codes_a.shape[0], devices
    )
    parts = lax.all_to_all(sums, AXES, 0, 0, tiled=True)
    aggregate = pl.pallas_call(
        functools.partial(ratio_body, ns * codes_a.shape[0]),
        out_shape=jax.ShapeDtypeStruct((2, P_SIZE), jnp.float32),
        in_specs=[pl.BlockSpec(memory_space=pltpu.VMEM)],
        out_specs=pl.BlockSpec(memory_space=pltpu.VMEM),
        compiler_params=pltpu.CompilerParams(vmem_limit_bytes=2**20),
        name="ratios",
    )(parts)
    return first_order, total_order, aggregate


def solution(mesh):
    placed = (P("gx", "gy"), P("gx", "gy"), P("gx", "gy"), P("sa", None), P("sa", None))
    return jax.shard_map(
        local,
        mesh=mesh,
        in_specs=placed,
        out_specs=(P(None, "gx", ("gy", "sa")), P(None, "gx", ("gy", "sa")), P()),
        check_vma=False,
    )
```
